32 devices in a mesh: stn: 8 (over z, x), tm: 4 (over y, core).
Axes of the slice: x: 2, y: 2, z: 4, core: 2. Of those that a mesh axis runs over, the one named last changes fastest.
Arguments:
- voltages: bfloat16 [2, 512, 262144], P(None, 'stn', 'tm'), may hold values from -6 to 6
- delays: int32 [512], P('stn'), may hold values from 0 to 2048, as said below
- fringe: int32 [512], P('stn'), may hold values from 0 to 4095
- fringe_rate: int32 [512], P('stn'), may hold values from 0 to 4095
- filter_taps: float32 [16, 1024], replicated, may hold values from -1.5 to 1.5
Outputs:
- vis_real: float32 [1024, 512, 512], P(('stn', 'tm'))
- vis_imag: float32 [1024, 512, 512], P(('stn', 'tm'))
The draws below stay inside these ranges and needn't reach their ends.
Inputs may be any that keep to these rules, and one draw needn't show every extreme that they name: `delays`: the largest delay over all stations is exactly 2048.
All inputs are finite; a program needn't handle non-finite values.
Results may differ from the reference program's by a relative error of at most 0.0066.
Values may be sent and summed in bfloat16 or wider, within the bound.
A program may use at most 448 MiB of HBM per device.

```python
import math
import jax
import jax.numpy as jnp
from jax import lax

S = 512
C = 1024
P_SIZE = 16
Q = 4096
TIME = 262144
DMAX = 2048


def draw_delays(key, part):
    key_values, key_place = jax.random.split(jax.random.fold_in(key, 7))
    values = jax.random.randint(key_values, (S,), 0, DMAX + 1)
    position = jax.random.randint(key_place, (), 0, S)
    return values.at[position].set(DMAX).astype(jnp.int32)


def set_ends(drawn, key, low, top_value):
    dims = drawn.shape
    spot = [jax.random.randint(jax.random.fold_in(key, axis), (), 0, dims[axis]) for axis in range(len(dims))]
    drawn = drawn.at[tuple(spot)].set(low)
    longest = dims.index(max(dims))
    spot[longest] = (spot[longest] + 1) % dims[longest]
    return drawn.at[tuple(spot)].set(top_value)


def levels(own_key, shape, cuts, least, high):
    loudness, own = 1.0, jax.random.fold_in(own_key, 6)
    for dim, shards_of in cuts:
        draws = jnp.exp(jax.random.uniform(jax.random.fold_in(own, dim), (shards_of,), jnp.float32, least / len(cuts), high / len(cuts)))
        loudness = loudness * jnp.repeat(draws, shape[dim] // shards_of).reshape([-1 if axis == dim else 1 for axis in range(len(shape))])
    return loudness


def scatter_about(own_key, dims, spread, most, cuts=(), kind=jnp.bfloat16):
    drawn = spread * jax.random.normal(own_key, dims, jnp.float32)
    if cuts:
        drawn = drawn * levels(own_key, dims, cuts, -0.22, 0.18)
    return jnp.clip(drawn, -most, most).astype(kind)


def setup_inputs(seed: int = 0) -> dict:
    key_list = jax.random.split(jax.random.key(seed), 6)
    voltages = scatter_about(key_list[0], (2, S, TIME), 1.0, 6.0, ((1, 8), (2, 4)))
    delays = draw_delays(jax.random.fold_in(key_list[5], 71), 0)
    fringe = set_ends(jax.random.randint(key_list[2], (S,), 0, Q), jax.random.fold_in(key_list[2], 1), 0, Q - 1).astype(jnp.int32)
    fringe_rate = set_ends(jax.random.randint(key_list[3], (S,), 0, Q), jax.random.fold_in(key_list[3], 1), 0, Q - 1).astype(jnp.int32)
    filter_taps = scatter_about(key_list[4], (P_SIZE, C), 0.25, 1.5, (), jnp.float32)
    return {"voltages": voltages, "delays": delays, "fringe": fringe, "fringe_rate": fringe_rate, "filter_taps": filter_taps}


TWO_PI = 2.0 * math.pi

def dft_tables(table_size):
    column = jnp.arange(table_size, dtype=jnp.int32)
    product = column[:, None] * column[None, :] % table_size
    angles = product.astype(jnp.float32) * (TWO_PI / table_size)
    return (jnp.cos(angles).astype(jnp.bfloat16), jnp.sin(angles).astype(jnp.bfloat16))

def transform(weighted_part, table):
    return jnp.einsum('smn,nc->csm', weighted_part.astype(jnp.float32), table.astype(jnp.float32), precision=lax.Precision.HIGHEST)

def channelize(delayed, filter_taps, fringe, fringe_rate, spectra, tables):
    stations = delayed.shape[1]
    blocks = delayed.reshape(2, stations, spectra + P_SIZE - 1, C)
    summed = jnp.zeros((2, stations, spectra, C), jnp.float32)
    for tap_index in range(P_SIZE):
        summed = summed + filter_taps[tap_index] * blocks[:, :, tap_index:tap_index + spectra].astype(jnp.float32)
    weighted = summed.astype(jnp.bfloat16)
    cosine_table, sine_table = tables
    inverse_root = 1.0 / math.sqrt(C)
    real_part = (transform(weighted[0], cosine_table) + transform(weighted[1], sine_table)) * inverse_root
    imag_part = (transform(weighted[1], cosine_table) - transform(weighted[0], sine_table)) * inverse_root
    channel = jnp.arange(C, dtype=jnp.int32)
    phase_index = (fringe[None, :] + fringe_rate[None, :] * channel[:, None]) % Q
    rotation = phase_index.astype(jnp.float32) * (TWO_PI / Q)
    rot_cos = jnp.cos(rotation)[:, :, None]
    rot_sin = jnp.sin(rotation)[:, :, None]
    out_real = real_part * rot_cos - imag_part * rot_sin
    out_imag = real_part * rot_sin + imag_part * rot_cos
    return jnp.stack([out_real, out_imag], axis=2).astype(jnp.bfloat16)

def reference(voltages, delays, fringe, fringe_rate, filter_taps):
    spectra = TIME // C
    padded = jnp.concatenate([jnp.zeros((2, S, DMAX), jnp.bfloat16), voltages, jnp.zeros((2, S, (P_SIZE - 1) * C), jnp.bfloat16)], axis=2)
    length = TIME + (P_SIZE - 1) * C
    tables = dft_tables(C)

    def select_window(station_row, delay_value):
        return lax.dynamic_slice_in_dim(station_row, (DMAX - delay_value).astype(jnp.int32), length, 1)

    def one_block(block_index):
        start = (block_index * 16).astype(jnp.int32)
        station_rows = lax.dynamic_slice_in_dim(padded, start, 16, 1)
        block_delays = lax.dynamic_slice_in_dim(delays, start, 16, 0)
        block_fringe = lax.dynamic_slice_in_dim(fringe, start, 16, 0)
        block_rate = lax.dynamic_slice_in_dim(fringe_rate, start, 16, 0)
        delayed = jax.vmap(select_window, in_axes=(1, 0), out_axes=1)(station_rows, block_delays)
        return channelize(delayed, filter_taps, block_fringe, block_rate, spectra, tables)
    stacked = lax.map(one_block, jnp.arange(S // 16, dtype=jnp.int32))

    def one_channel_block(block_index):
        start = (block_index * 8).astype(jnp.int32)
        chosen = lax.dynamic_slice_in_dim(stacked, start, 8, 1)
        left_rows = jnp.transpose(chosen, (1, 0, 2, 3, 4)).reshape(8, S, 2 * spectra).astype(jnp.float32)
        swapped = jnp.concatenate([left_rows[..., spectra:], -left_rows[..., :spectra]], axis=-1)
        gram_real = jnp.einsum('csk,cdk->csd', left_rows, left_rows, precision=lax.Precision.HIGHEST)
        gram_imag = jnp.einsum('csk,cdk->csd', swapped, left_rows, precision=lax.Precision.HIGHEST)
        return (gram_real * (1.0 / spectra), gram_imag * (1.0 / spectra))
    vis_real, vis_imag = lax.map(one_channel_block, jnp.arange(C // 8, dtype=jnp.int32))
    return (vis_real.reshape(C, S, S), vis_imag.reshape(C, S, S))
```

```python
import functools
import math

import jax
import jax.numpy as jnp
import numpy as np
from jax import lax
from jax.experimental import pallas as pl
from jax.experimental.pallas import tpu as pltpu
from jax.sharding import PartitionSpec as P

C = 1024
P_SIZE = 16
Q = 4096
DMAX = 2048

TWO_PI = 2.0 * math.pi
LANES = 128
GROUP = 16
CHUNK = 256
EARLY = DMAX // C
LATE = P_SIZE - 1
WIDE = P_SIZE + EARLY
MESH = pl.DeviceIdType.MESH


def dft_table():
    column = np.arange(C, dtype=np.int64)
    angles = (column[:, None] * column[None, :] % C).astype(np.float32) * np.float32(TWO_PI / C)
    both = np.concatenate([np.cos(angles), np.sin(angles)], axis=1)
    return both.astype(jnp.bfloat16)


def turn_table(delays, fringe, fringe_rate, groups):
    channel = jnp.arange(C, dtype=jnp.int32)
    rate = (fringe_rate - (Q // C) * delays).reshape(groups, 1, GROUP)
    phase_index = (fringe.reshape(groups, 1, GROUP) + rate * channel[None, :, None]) % Q
    rotation = phase_index.astype(jnp.float32) * (TWO_PI / Q)
    inverse_root = 1.0 / math.sqrt(C)
    return jnp.concatenate([jnp.cos(rotation), jnp.sin(rotation)], axis=2) * inverse_root


def roll_left(tiles, step, chosen):
    count = len(tiles)
    if step >= LANES:
        moved = [tiles[(i + step // LANES) % count] for i in range(count)]
    else:
        lane = lax.broadcasted_iota(jnp.int32, tiles[0].shape, 1)
        turned = [pltpu.roll(tile, LANES - step, 1) for tile in tiles]
        moved = [jnp.where(lane < LANES - step, turned[i], turned[(i + 1) % count]) for i in range(count)]
    return [jnp.where(chosen, new, old) for new, old in zip(moved, tiles)]


def spread_kernel(
    stn_count, tm_count, volt, delay_ref, taps_ref, table_ref, turn_ref, recv,
    x, taps, mixed, rows, flat, send, load_sem, early_sems, late_sems, send_sems, recv_sems, own_sems,
):
    stn, tm = lax.axis_index("stn"), lax.axis_index("tm")
    me = stn * tm_count + tm
    devices = stn_count * tm_count
    groups = x.shape[0]
    samples = volt.shape[2]
    spectra = samples // C
    each = C // devices
    per_chunk = CHUNK // each
    chunks = C // CHUNK
    tiles = C // LANES

    def load(g):
        return pltpu.make_async_copy(
            volt.at[:, pl.ds(g * GROUP, GROUP), :],
            x.at[g, :, :, pl.ds(EARLY * C, samples)],
            load_sem.at[g],
        )

    def early(g):
        return pltpu.make_async_remote_copy(
            volt.at[:, pl.ds(g * GROUP, GROUP), pl.ds(samples - EARLY * C, EARLY * C)],
            x.at[g, :, :, pl.ds(0, EARLY * C)],
            early_sems.at[0, g], early_sems.at[1, g],
            device_id=(stn, lax.rem(tm + 1, tm_count)), device_id_type=MESH,
        )

    def late(g):
        return pltpu.make_async_remote_copy(
            volt.at[:, pl.ds(g * GROUP, GROUP), pl.ds(0, LATE * C)],
            x.at[g, :, :, pl.ds(EARLY * C + samples, LATE * C)],
            late_sems.at[0, g], late_sems.at[1, g],
            device_id=(stn, lax.rem(tm + tm_count - 1, tm_count)), device_id_type=MESH,
        )

    def spread(g, slot, mask):
        other = jnp.bitwise_xor(me, mask)
        return pltpu.make_async_remote_copy(
            send.at[slot, pl.ds(other * each, each)],
            recv.at[stn, tm, g],
            send_sems.at[g, mask], recv_sems.at[g, mask],
            device_id=(other // tm_count, lax.rem(other, tm_count)), device_id_type=MESH,
        )

    def keep(g, slot):
        return pltpu.make_async_copy(send.at[slot, pl.ds(me * each, each)], recv.at[stn, tm, g], own_sems.at[g])

    for g in range(groups):
        load(g).start()

    barrier = pltpu.get_barrier_semaphore()

    def greet(mask, carry):
        other = jnp.bitwise_xor(me, mask)
        pl.semaphore_signal(
            barrier, inc=1, device_id=(other // tm_count, lax.rem(other, tm_count)), device_id_type=MESH
        )
        return carry

    lax.fori_loop(1, devices, greet, 0)
    pl.semaphore_wait(barrier, devices - 1)

    @pl.when(tm > 0)
    def _():
        for g in range(groups):
            late(g).start()

    @pl.when(tm < tm_count - 1)
    def _():
        for g in range(groups):
            early(g).start()

    @pl.when(tm == 0)
    def _():
        x[:, :, :, 0 : EARLY * C] = jnp.zeros((groups, 2, GROUP, EARLY * C), x.dtype)

    @pl.when(tm == tm_count - 1)
    def _():
        for g in range(groups):
            x[g, :, :, EARLY * C + samples :] = jnp.zeros((2, GROUP, LATE * C), x.dtype)

    for edge in list(range(EARLY)) + list(range(EARLY + P_SIZE, 2 * EARLY + P_SIZE)):
        taps[edge] = jnp.zeros((GROUP, C), jnp.float32)

    def one_group(g, carry):
        slot = lax.rem(g, 2)

        for half in range(0, GROUP, 8):
            delay = delay_ref[pl.ds(pl.multiple_of(g * GROUP + half, 8), 8), :]

            def one_tap(tap, carry):
                own = taps_ref[tap]
                line = [jnp.broadcast_to(own[i : i + 1], (8, LANES)) for i in range(tiles)]
                step = 1
                while step < C:
                    line = roll_left(line, step, jnp.bitwise_and(delay, step) != 0)
                    step *= 2
                for i in range(tiles):
                    taps[EARLY + tap, half : half + 8, i * LANES : (i + 1) * LANES] = line[i]
                return carry

            lax.fori_loop(0, P_SIZE, one_tap, 0)

        load(g).wait()

        @pl.when(tm > 0)
        def _():
            early(g).wait_recv()

        @pl.when(tm < tm_count - 1)
        def _():
            late(g).wait_recv()

        def weigh(index, carry):
            part = index // tiles
            offset = pl.multiple_of(lax.rem(index, tiles) * LANES, LANES)
            lane = offset + lax.broadcasted_iota(jnp.int32, (8, LANES), 1)
            for half in range(0, GROUP, 8):
                delay = delay_ref[pl.ds(pl.multiple_of(g * GROUP + half, 8), 8), :]
                behind = delay // C + jnp.where(lane >= C - lax.rem(delay, C), 1, 0)
                rolled = [taps[q, half : half + 8, pl.ds(offset, LANES)] for q in range(WIDE + EARLY)]
                factor = []
                for q in range(WIDE):
                    value = rolled[q]
                    for back in range(1, EARLY + 1):
                        value = jnp.where(behind == back, rolled[q + back], value)
                    factor.append(value)
                for base in range(0, spectra, 16):
                    frames = [
                        x[g, part, :, pl.ds(pl.multiple_of((base + j) * C + offset, LANES), LANES)].astype(
                            jnp.float32
                        )[half : half + 8]
                        for j in range(16 + WIDE - 1)
                    ]
                    for m in range(16):
                        total = factor[0] * frames[m]
                        for q in range(1, WIDE):
                            total = total + factor[q] * frames[m + q]
                        mixed[pl.ds(half * spectra + base + m, 8, stride=spectra), :] = total
            sign = jnp.where(part == 0, -1.0, 1.0)
            same = pl.multiple_of(part * C + offset, LANES)
            cross = pl.multiple_of((1 - part) * C + offset, LANES)
            for s in range(GROUP):
                value = mixed[s * spectra : (s + 1) * spectra, :]
                first = s * 2 * spectra
                rows[first : first + spectra, pl.ds(same, LANES)] = value.astype(jnp.bfloat16)
                rows[first + spectra : first + 2 * spectra, pl.ds(cross, LANES)] = (value * sign).astype(jnp.bfloat16)
            return carry

        lax.fori_loop(0, 2 * tiles, weigh, 0)

        @pl.when(g >= 2)
        def _():
            def gone(mask, carry):
                spread(g - 2, slot, mask).wait_send()
                return carry

            lax.fori_loop(1, devices, gone, 0)
            keep(g - 2, slot).wait()

        def one_chunk(index, carry):
            away = jnp.where(index == 0, 2, jnp.where(index == 1, 1, jnp.where(index == 2, 3, 0)))
            chunk = jnp.bitwise_xor(me // per_chunk, away)
            first = pl.multiple_of(chunk * CHUNK, CHUNK)
            left = table_ref[pl.ds(first, CHUNK), :]
            width = 2 * spectra
            side = jnp.where(lax.broadcasted_iota(jnp.int32, (CHUNK, width), 1) < spectra, -1.0, 1.0)
            for s in range(0, GROUP, 2):
                product = lax.dot_general(
                    left, rows[s * width : (s + 2) * width, :], (((1,), (1,)), ((), ())),
                    preferred_element_type=jnp.float32,
                )
                for station in (s, s + 1):
                    value = product[:, (station - s) * width : (station - s + 1) * width]
                    cosine = turn_ref[g, pl.ds(first, CHUNK), station : station + 1]
                    sine = turn_ref[g, pl.ds(first, CHUNK), GROUP + station : GROUP + station + 1]
                    turned = value * cosine + pltpu.roll(value, spectra, 1) * (side * sine)
                    for c in range(0, CHUNK, 8):
                        flat[pl.ds(c * GROUP + station, 8, stride=GROUP), :] = turned[c : c + 8]

            def pack(block, carry):
                value = flat[pl.ds(pl.multiple_of(block * 128, 128), 128), :].astype(jnp.bfloat16)
                send[slot, pl.ds(first + block * (128 // GROUP), 128 // GROUP)] = value.reshape(
                    128 // GROUP, GROUP, width
                )
                return carry

            lax.fori_loop(0, CHUNK * GROUP // 128, pack, 0)

            def go(i, carry):
                mask = away * per_chunk + i

                @pl.when(mask > 0)
                def _():
                    spread(g, slot, mask).start()

                @pl.when(mask == 0)
                def _():
                    keep(g, slot).start()

                return carry

            lax.fori_loop(0, per_chunk, go, 0)
            return carry

        lax.fori_loop(0, chunks, one_chunk, 0)
        return carry

    lax.fori_loop(0, groups, one_group, 0)

    for g in range(groups):
        if g >= groups - 2:
            def gone(mask, carry):
                spread(g, g % 2, mask).wait_send()
                return carry

            lax.fori_loop(1, devices, gone, 0)
            keep(g, g % 2).wait()

        def come(mask, carry):
            spread(g, g % 2, mask).wait_recv()
            return carry

        lax.fori_loop(1, devices, come, 0)

    @pl.when(tm > 0)
    def _():
        for g in range(groups):
            late(g).wait_send()

    @pl.when(tm < tm_count - 1)
    def _():
        for g in range(groups):
            early(g).wait_send()


def spread_spectra(voltages, delays, filter_taps, turn, stn_count, tm_count):
    stations, samples = voltages.shape[1:]
    spectra = samples // C
    groups = stations // GROUP
    devices = stn_count * tm_count
    each = C // devices
    width = 2 * spectra
    vmem = pl.BlockSpec(memory_space=pltpu.VMEM)
    hbm = pl.BlockSpec(memory_space=pl.ANY)
    return pl.pallas_call(
        functools.partial(spread_kernel, stn_count, tm_count),
        in_specs=[hbm, vmem, vmem, vmem, vmem],
        out_specs=hbm,
        out_shape=jax.ShapeDtypeStruct((stn_count, tm_count, groups, each, GROUP, width), jnp.bfloat16),
        scratch_shapes=[
            pltpu.VMEM((groups, 2, GROUP, (EARLY + LATE) * C + samples), jnp.bfloat16),
            pltpu.VMEM((P_SIZE + 2 * EARLY, GROUP, C), jnp.float32),
            pltpu.VMEM((GROUP * spectra, LANES), jnp.float32),
            pltpu.VMEM((GROUP * width, 2 * C), jnp.bfloat16),
            pltpu.VMEM((CHUNK * GROUP, width), jnp.float32),
            pltpu.VMEM((2, C, GROUP, width), jnp.bfloat16),
            pltpu.SemaphoreType.DMA((groups,)),
            pltpu.SemaphoreType.DMA((2, groups)),
            pltpu.SemaphoreType.DMA((2, groups)),
            pltpu.SemaphoreType.DMA((groups, devices)),
            pltpu.SemaphoreType.DMA((groups, devices)),
            pltpu.SemaphoreType.DMA((groups,)),
        ],
        compiler_params=pltpu.CompilerParams(
            collective_id=0, has_side_effects=True, vmem_limit_bytes=60 * 1024 * 1024
        ),
    )(voltages, jnp.broadcast_to(delays[:, None], (stations, LANES)), filter_taps.reshape(P_SIZE, C // LANES, LANES), jnp.asarray(dft_table()), turn)


def gram_kernel(scale, spectra_ref, real_ref, imag_ref):
    stn_count, tm_count, groups, channels, size, width = spectra_ref.shape
    whole = stn_count * groups * size
    lane = lax.broadcasted_iota(jnp.int32, (whole, width), 1)
    last = (((1,), (1,)), ((), ()))
    for channel in range(channels):
        pieces, turned_pieces = [], []
        for source in range(tm_count):
            piece = spectra_ref[:, source, :, channel].reshape(whole, width)
            turned = pltpu.roll(piece.astype(jnp.float32), width // 2, 1)
            pieces.append(piece)
            turned_pieces.append(jnp.where(lane < width // 2, turned, -turned).astype(jnp.bfloat16))
        rows = jnp.concatenate(pieces, axis=1)
        swapped = jnp.concatenate(turned_pieces, axis=1)
        real_ref[channel] = lax.dot_general(rows, rows, last, preferred_element_type=jnp.float32) * scale
        imag_ref[channel] = lax.dot_general(swapped, rows, last, preferred_element_type=jnp.float32) * scale


def grams(received, scale):
    stn_count, tm_count, groups, channels, size, width = received.shape
    whole = stn_count * groups * size
    step = 2
    result = jax.ShapeDtypeStruct((channels, whole, whole), jnp.float32)
    return pl.pallas_call(
        functools.partial(gram_kernel, scale),
        grid=(channels // step,),
        in_specs=[pl.BlockSpec((stn_count, tm_count, groups, step, size, width), lambda c: (0, 0, 0, c, 0, 0))],
        out_specs=[pl.BlockSpec((step, whole, whole), lambda c: (c, 0, 0))] * 2,
        out_shape=[result, result],
        compiler_params=pltpu.CompilerParams(vmem_limit_bytes=60 * 1024 * 1024),
    )(received)


def local(stn_count, tm_count, voltages, delays, fringe, fringe_rate, filter_taps):
    spectra = voltages.shape[2] // C
    groups = voltages.shape[1] // GROUP
    turn = turn_table(delays, fringe, fringe_rate, groups)
    received = spread_spectra(voltages, delays, filter_taps, turn, stn_count, tm_count)
    real, imag = grams(received, 1.0 / (spectra * tm_count))
    return (real, imag)


def solution(mesh):
    return jax.shard_map(
        functools.partial(local, mesh.shape["stn"], mesh.shape["tm"]),
        mesh=mesh,
        in_specs=(P(None, "stn", "tm"), P("stn"), P("stn"), P("stn"), P()),
        out_specs=(P(("stn", "tm"), None, None), P(("stn", "tm"), None, None)),
        check_vma=False,
    )
```

```python
import functools
import math

import jax
import jax.numpy as jnp
import numpy as np
from jax import lax
from jax.experimental import pallas as pl
from jax.experimental.pallas import tpu as pltpu
from jax.sharding import PartitionSpec as P

C = 1024
P_SIZE = 16
Q = 4096
DMAX = 2048

TWO_PI = 2.0 * math.pi
LANES = 128
GROUP = 16
CHUNK = 256
STEP = 16
EARLY = DMAX // C
LATE = P_SIZE - 1
WIDE = P_SIZE + EARLY
MESH = pl.DeviceIdType.MESH


def dft_table():
    column = np.arange(C, dtype=np.int64)
    angles = (column[:, None] * column[None, :] % C).astype(np.float32) * np.float32(TWO_PI / C)
    both = np.concatenate([np.cos(angles), np.sin(angles)], axis=1)
    return both.astype(jnp.bfloat16)


def roll_left(tiles, amount):
    count = len(tiles)
    lane = lax.broadcasted_iota(jnp.int32, tiles[0].shape, 1)
    within = jnp.bitwise_and(amount, LANES - 1)
    source = jnp.bitwise_and(lane + within, LANES - 1)
    turned = [jnp.take_along_axis(tile, source, axis=1) for tile in tiles]
    line = [jnp.where(lane < LANES - within, turned[i], turned[(i + 1) % count]) for i in range(count)]
    step = 1
    while step < count:
        chosen = jnp.bitwise_and(amount, step * LANES) != 0
        line = [jnp.where(chosen, line[(i + step) % count], line[i]) for i in range(count)]
        step *= 2
    return line


def by_station(ref, first, index, shape):
    value = jnp.zeros(shape, jnp.int32)
    for i in range(GROUP):
        value = jnp.where(index == i, ref[first + i], value)
    return value


def spread_kernel(
    stn_count, tm_count, volt, table_ref, delay_ref, fringe_ref, rate_ref, taps_ref, recv,
    x, table, taps, lag, turn, mixed, rows, flat, send,
    load_sem, table_sem, early_sems, late_sems, send_sems, recv_sems, own_sems,
):
    stn, tm = lax.axis_index("stn"), lax.axis_index("tm")
    me = stn * tm_count + tm
    devices = stn_count * tm_count
    groups = x.shape[0]
    samples = volt.shape[2]
    spectra = samples // C
    each = C // devices
    per_chunk = CHUNK // each
    chunks = C // CHUNK
    tiles = C // LANES

    def load(g):
        return pltpu.make_async_copy(
            volt.at[:, pl.ds(g * GROUP, GROUP), :],
            x.at[g, :, :, pl.ds(EARLY * C, samples)],
            load_sem.at[g],
        )

    def early(g):
        return pltpu.make_async_remote_copy(
            volt.at[:, pl.ds(g * GROUP, GROUP), pl.ds(samples - EARLY * C, EARLY * C)],
            x.at[g, :, :, pl.ds(0, EARLY * C)],
            early_sems.at[0, g], early_sems.at[1, g],
            device_id=(stn, lax.rem(tm + 1, tm_count)), device_id_type=MESH,
        )

    def late(g):
        return pltpu.make_async_remote_copy(
            volt.at[:, pl.ds(g * GROUP, GROUP), pl.ds(0, LATE * C)],
            x.at[g, :, :, pl.ds(EARLY * C + samples, LATE * C)],
            late_sems.at[0, g], late_sems.at[1, g],
            device_id=(stn, lax.rem(tm + tm_count - 1, tm_count)), device_id_type=MESH,
        )

    def spread(g, mask):
        other = jnp.bitwise_xor(me, mask)
        return pltpu.make_async_remote_copy(
            send.at[g, pl.ds(other * each, each)],
            recv.at[stn, tm, g],
            send_sems.at[g, mask], recv_sems.at[g, mask],
            device_id=(other // tm_count, lax.rem(other, tm_count)), device_id_type=MESH,
        )

    def keep(g):
        return pltpu.make_async_copy(send.at[g, pl.ds(me * each, each)], recv.at[stn, tm, g], own_sems.at[g])

    whole_table = pltpu.make_async_copy(table_ref, table, table_sem)
    load(0).start()
    whole_table.start()
    for g in range(1, groups):
        load(g).start()

    barrier = pltpu.get_barrier_semaphore()

    def greet(mask, carry):
        other = jnp.bitwise_xor(me, mask)
        pl.semaphore_signal(
            barrier, inc=1, device_id=(other // tm_count, lax.rem(other, tm_count)), device_id_type=MESH
        )
        return carry

    lax.fori_loop(1, devices, greet, 0)

    def reach(g):
        @pl.when(tm < tm_count - 1)
        def _():
            early(g).start()

        @pl.when(tm > 0)
        def _():
            late(g).start()

    def prepare(g):
        sub = lax.broadcasted_iota(jnp.int32, (8, LANES), 0)
        for half in range(0, GROUP, 8):
            delay = by_station(delay_ref, g * GROUP, sub + half, (8, LANES))
            lag[half : half + 8, :] = delay
            for tap in range(P_SIZE):
                line = [
                    jnp.broadcast_to(taps_ref[tap : tap + 1, i * LANES : (i + 1) * LANES], (8, LANES))
                    for i in range(tiles)
                ]
                line = roll_left(line, jnp.bitwise_and(delay, C - 1))
                for i in range(tiles):
                    taps[EARLY + tap, half : half + 8, i * LANES : (i + 1) * LANES] = line[i]
        lane = lax.broadcasted_iota(jnp.int32, (8, LANES), 1)
        which = jnp.bitwise_and(lane, GROUP - 1)
        start = by_station(fringe_ref, g * GROUP, which, (8, LANES)) - jnp.where(lane < GROUP, 0, Q // 4)
        rate = by_station(rate_ref, g * GROUP, which, (8, LANES)) - (Q // C) * by_station(
            delay_ref, g * GROUP, which, (8, LANES)
        )

        def angle(block, carry):
            first = pl.multiple_of(block * 32, 32)
            for more in range(0, 32, 8):
                phase_index = jnp.bitwise_and(start + rate * (sub + first + more), Q - 1)
                turn[pl.ds(first + more, 8), :] = jnp.cos(phase_index.astype(jnp.float32) * (TWO_PI / Q)) * (
                    1.0 / math.sqrt(C)
                )
            return carry

        lax.fori_loop(0, C // 32, angle, 0)

    for edge in list(range(EARLY)) + list(range(EARLY + P_SIZE, 2 * EARLY + P_SIZE)):
        taps[edge] = jnp.zeros((GROUP, C), jnp.float32)

    @pl.when(tm == 0)
    def _():
        x[:, :, :, 0 : EARLY * C] = jnp.zeros((groups, 2, GROUP, EARLY * C), x.dtype)

    @pl.when(tm == tm_count - 1)
    def _():
        for g in range(groups):
            x[g, :, :, EARLY * C + samples :] = jnp.zeros((2, GROUP, LATE * C), x.dtype)

    pl.semaphore_wait(barrier, devices - 1)
    reach(0)

    def one_group(g, carry):
        prepare(g)
        load(g).wait()

        @pl.when(tm > 0)
        def _():
            early(g).wait_recv()

        def weigh(low, high, index, carry):
            part = index // tiles
            offset = pl.multiple_of(lax.rem(index, tiles) * LANES, LANES)
            lane = offset + lax.broadcasted_iota(jnp.int32, (8, LANES), 1)
            for half in range(0, GROUP, 8):
                delay = lag[half : half + 8, :]
                behind = lax.shift_right_logical(delay, C.bit_length() - 1) + jnp.where(
                    lane >= C - jnp.bitwise_and(delay, C - 1), 1, 0
                )
                rolled = [taps[q, half : half + 8, pl.ds(offset, LANES)] for q in range(WIDE + EARLY)]
                factor = []
                for q in range(WIDE):
                    value = rolled[q]
                    for back in range(1, EARLY + 1):
                        value = jnp.where(behind == back, rolled[q + back], value)
                    factor.append(value)
                for base in range(low, high, STEP):
                    frames = [
                        x[g, part, :, pl.ds(pl.multiple_of((base + j) * C + offset, LANES), LANES)].astype(
                            jnp.float32
                        )[half : half + 8]
                        for j in range(STEP + WIDE - 1)
                    ]
                    for m in range(STEP):
                        total = factor[0] * frames[m]
                        for q in range(1, WIDE):
                            total = total + factor[q] * frames[m + q]
                        mixed[pl.ds(half * spectra + base + m, 8, stride=spectra), :] = total
            sign = jnp.where(part == 0, -1.0, 1.0)
            same = pl.multiple_of(part * C + offset, LANES)
            cross = pl.multiple_of((1 - part) * C + offset, LANES)
            for s in range(GROUP):
                value = mixed[s * spectra + low : s * spectra + high, :]
                first = s * 2 * spectra
                rows[first + low : first + high, pl.ds(same, LANES)] = value.astype(jnp.bfloat16)
                rows[first + spectra + low : first + spectra + high, pl.ds(cross, LANES)] = (value * sign).astype(jnp.bfloat16)
            return carry

        inner = max(0, (spectra - LATE) // 16 * 16)
        if inner:
            lax.fori_loop(0, 2 * tiles, functools.partial(weigh, 0, inner), 0)

        @pl.when(tm < tm_count - 1)
        def _():
            late(g).wait_recv()

        lax.fori_loop(0, 2 * tiles, functools.partial(weigh, inner, spectra), 0)

        @pl.when(g == 0)
        def _():
            whole_table.wait()

        @pl.when(g + 1 < groups)
        def _():
            reach(g + 1)

        def one_chunk(index, carry):
            away = jnp.where(index == 0, 2, jnp.where(index == 1, 1, jnp.where(index == 2, 3, 0)))
            chunk = jnp.bitwise_xor(me // per_chunk, away)
            first = pl.multiple_of(chunk * CHUNK, CHUNK)
            left = table[pl.ds(first, CHUNK), :]
            width = 2 * spectra
            side = jnp.where(lax.broadcasted_iota(jnp.int32, (CHUNK, width), 1) < spectra, -1.0, 1.0)
            for s in range(0, GROUP, 2):
                product = lax.dot_general(
                    left, rows[s * width : (s + 2) * width, :], (((1,), (1,)), ((), ())),
                    preferred_element_type=jnp.float32,
                )
                for station in (s, s + 1):
                    value = product[:, (station - s) * width : (station - s + 1) * width]
                    cosine = turn[pl.ds(first, CHUNK), station : station + 1]
                    sine = turn[pl.ds(first, CHUNK), GROUP + station : GROUP + station + 1]
                    turned = value * cosine + pltpu.roll(value, spectra, 1) * (side * sine)
                    for c in range(0, CHUNK, 8):
                        flat[pl.ds(c * GROUP + station, 8, stride=GROUP), :] = turned[c : c + 8]

            def pack(block, carry):
                value = flat[pl.ds(pl.multiple_of(block * 128, 128), 128), :].astype(jnp.bfloat16)
                send[g, pl.ds(first + block * (128 // GROUP), 128 // GROUP)] = value.reshape(
                    128 // GROUP, GROUP, width
                )
                return carry

            lax.fori_loop(0, CHUNK * GROUP // 128, pack, 0)

            def go(i, carry):
                mask = away * per_chunk + i

                @pl.when(mask > 0)
                def _():
                    spread(g, mask).start()

                @pl.when(mask == 0)
                def _():
                    keep(g).start()

                return carry

            lax.fori_loop(0, per_chunk, go, 0)
            return carry

        lax.fori_loop(0, chunks, one_chunk, 0)
        return carry

    lax.fori_loop(0, groups, one_group, 0)

    for g in range(groups):
        keep(g).wait()

        def come(mask, carry):
            spread(g, mask).wait()
            return carry

        lax.fori_loop(1, devices, come, 0)

    @pl.when(tm > 0)
    def _():
        for g in range(groups):
            late(g).wait_send()

    @pl.when(tm < tm_count - 1)
    def _():
        for g in range(groups):
            early(g).wait_send()


def spread_spectra(voltages, delays, fringe, fringe_rate, filter_taps, stn_count, tm_count):
    stations, samples = voltages.shape[1:]
    spectra = samples // C
    groups = stations // GROUP
    devices = stn_count * tm_count
    each = C // devices
    width = 2 * spectra
    vmem = pl.BlockSpec(memory_space=pltpu.VMEM)
    smem = pl.BlockSpec(memory_space=pltpu.SMEM)
    hbm = pl.BlockSpec(memory_space=pl.ANY)
    return pl.pallas_call(
        functools.partial(spread_kernel, stn_count, tm_count),
        in_specs=[hbm, hbm, smem, smem, smem, vmem],
        out_specs=hbm,
        out_shape=jax.ShapeDtypeStruct((stn_count, tm_count, groups, each, GROUP, width), jnp.bfloat16),
        scratch_shapes=[
            pltpu.VMEM((groups, 2, GROUP, (EARLY + LATE) * C + samples), jnp.bfloat16),
            pltpu.VMEM((C, 2 * C), jnp.bfloat16),
            pltpu.VMEM((P_SIZE + 2 * EARLY, GROUP, C), jnp.float32),
            pltpu.VMEM((GROUP, LANES), jnp.int32),
            pltpu.VMEM((C, LANES), jnp.float32),
            pltpu.VMEM((GROUP * spectra, LANES), jnp.float32),
            pltpu.VMEM((GROUP * width, 2 * C), jnp.bfloat16),
            pltpu.VMEM((CHUNK * GROUP, width), jnp.float32),
            pltpu.VMEM((groups, C, GROUP, width), jnp.bfloat16),
            pltpu.SemaphoreType.DMA((groups,)),
            pltpu.SemaphoreType.DMA,
            pltpu.SemaphoreType.DMA((2, groups)),
            pltpu.SemaphoreType.DMA((2, groups)),
            pltpu.SemaphoreType.DMA((groups, devices)),
            pltpu.SemaphoreType.DMA((groups, devices)),
            pltpu.SemaphoreType.DMA((groups,)),
        ],
        compiler_params=pltpu.CompilerParams(
            collective_id=0, has_side_effects=True, vmem_limit_bytes=60 * 1024 * 1024
        ),
    )(voltages, jnp.asarray(dft_table()), delays, fringe, fringe_rate, filter_taps)


def gram_kernel(scale, spectra_ref, real_ref, imag_ref):
    stn_count, tm_count, groups, channels, size, width = spectra_ref.shape
    whole = stn_count * groups * size
    lane = lax.broadcasted_iota(jnp.int32, (whole, width), 1)
    last = (((1,), (1,)), ((), ()))
    for channel in range(channels):
        pieces, turned_pieces = [], []
        for source in range(tm_count):
            piece = spectra_ref[:, source, :, channel].reshape(whole, width)
            turned = pltpu.roll(piece.astype(jnp.float32), width // 2, 1)
            pieces.append(piece)
            turned_pieces.append(jnp.where(lane < width // 2, turned, -turned).astype(jnp.bfloat16))
        rows = jnp.concatenate(pieces, axis=1)
        swapped = jnp.concatenate(turned_pieces, axis=1)
        real_ref[channel] = lax.dot_general(rows, rows, last, preferred_element_type=jnp.float32) * scale
        imag_ref[channel] = lax.dot_general(swapped, rows, last, preferred_element_type=jnp.float32) * scale


def grams(received, scale):
    stn_count, tm_count, groups, channels, size, width = received.shape
    whole = stn_count * groups * size
    step = 2
    result = jax.ShapeDtypeStruct((channels, whole, whole), jnp.float32)
    return pl.pallas_call(
        functools.partial(gram_kernel, scale),
        grid=(channels // step,),
        in_specs=[pl.BlockSpec((stn_count, tm_count, groups, step, size, width), lambda c: (0, 0, 0, c, 0, 0))],
        out_specs=[pl.BlockSpec((step, whole, whole), lambda c: (c, 0, 0))] * 2,
        out_shape=[result, result],
        compiler_params=pltpu.CompilerParams(vmem_limit_bytes=60 * 1024 * 1024),
    )(received)


def local(stn_count, tm_count, voltages, delays, fringe, fringe_rate, filter_taps):
    spectra = voltages.shape[2] // C
    received = spread_spectra(voltages, delays, fringe, fringe_rate, filter_taps, stn_count, tm_count)
    real, imag = grams(received, 1.0 / (spectra * tm_count))
    return (real, imag)


def solution(mesh):
    return jax.shard_map(
        functools.partial(local, mesh.shape["stn"], mesh.shape["tm"]),
        mesh=mesh,
        in_specs=(P(None, "stn", "tm"), P("stn"), P("stn"), P("stn"), P()),
        out_specs=(P(("stn", "tm"), None, None), P(("stn", "tm"), None, None)),
        check_vma=False,
    )
```

```python
import functools
import math

import jax
import jax.numpy as jnp
import numpy as np
from jax import lax
from jax.experimental import pallas as pl
from jax.experimental.pallas import tpu as pltpu
from jax.sharding import PartitionSpec as P

C = 1024
P_SIZE = 16
Q = 4096
DMAX = 2048

TWO_PI = 2.0 * math.pi
LANES = 128
GROUP = 16
CHUNK = 256
STEP = 16
EARLY = DMAX // C
LATE = P_SIZE - 1
WIDE = P_SIZE + EARLY
MESH = pl.DeviceIdType.MESH


def dft_table():
    column = np.arange(C, dtype=np.int64)
    angles = (column[:, None] * column[None, :] % C).astype(np.float32) * np.float32(TWO_PI / C)
    both = np.concatenate([np.cos(angles), np.sin(angles)], axis=1)
    return both.astype(jnp.bfloat16)


def roll_left(tiles, amount):
    count = len(tiles)
    lane = lax.broadcasted_iota(jnp.int32, tiles[0].shape, 1)
    within = jnp.bitwise_and(amount, LANES - 1)
    source = jnp.bitwise_and(lane + within, LANES - 1)
    turned = [jnp.take_along_axis(tile, source, axis=1) for tile in tiles]
    line = [jnp.where(lane < LANES - within, turned[i], turned[(i + 1) % count]) for i in range(count)]
    step = 1
    while step < count:
        chosen = jnp.bitwise_and(amount, step * LANES) != 0
        line = [jnp.where(chosen, line[(i + step) % count], line[i]) for i in range(count)]
        step *= 2
    return line


def by_station(ref, first, index, shape):
    value = jnp.zeros(shape, jnp.int32)
    for i in range(GROUP):
        value = jnp.where(index == i, ref[first + i], value)
    return value


def spread_kernel(
    stn_count, tm_count, volt, table_ref, delay_ref, fringe_ref, rate_ref, taps_ref, recv,
    x, table, taps, lag, turn, mixed, rows, flat, send,
    load_sem, table_sem, early_sems, late_sems, send_sems, recv_sems, own_sems,
):
    stn, tm = lax.axis_index("stn"), lax.axis_index("tm")
    me = stn * tm_count + tm
    devices = stn_count * tm_count
    groups = x.shape[0]
    samples = volt.shape[2]
    spectra = samples // C
    each = C // devices
    per_chunk = CHUNK // each
    chunks = C // CHUNK
    tiles = C // LANES
    apart = mixed.shape[0] // GROUP

    def load(g):
        return pltpu.make_async_copy(
            volt.at[:, pl.ds(g * GROUP, GROUP), :],
            x.at[g, :, :, pl.ds(EARLY * C, samples)],
            load_sem.at[g],
        )

    def early(g):
        return pltpu.make_async_remote_copy(
            volt.at[:, pl.ds(g * GROUP, GROUP), pl.ds(samples - EARLY * C, EARLY * C)],
            x.at[g, :, :, pl.ds(0, EARLY * C)],
            early_sems.at[0, g], early_sems.at[1, g],
            device_id=(stn, lax.rem(tm + 1, tm_count)), device_id_type=MESH,
        )

    def late(g):
        return pltpu.make_async_remote_copy(
            volt.at[:, pl.ds(g * GROUP, GROUP), pl.ds(0, LATE * C)],
            x.at[g, :, :, pl.ds(EARLY * C + samples, LATE * C)],
            late_sems.at[0, g], late_sems.at[1, g],
            device_id=(stn, lax.rem(tm + tm_count - 1, tm_count)), device_id_type=MESH,
        )

    def spread(g, mask):
        other = jnp.bitwise_xor(me, mask)
        return pltpu.make_async_remote_copy(
            send.at[g, pl.ds(other * each, each)],
            recv.at[stn, tm, g],
            send_sems.at[g, mask], recv_sems.at[g, mask],
            device_id=(other // tm_count, lax.rem(other, tm_count)), device_id_type=MESH,
        )

    def keep(g):
        return pltpu.make_async_copy(send.at[g, pl.ds(me * each, each)], recv.at[stn, tm, g], own_sems.at[g])

    whole_table = pltpu.make_async_copy(table_ref, table, table_sem)
    load(0).start()
    whole_table.start()
    for g in range(1, groups):
        load(g).start()

    barrier = pltpu.get_barrier_semaphore()

    def greet(mask, carry):
        other = jnp.bitwise_xor(me, mask)
        pl.semaphore_signal(
            barrier, inc=1, device_id=(other // tm_count, lax.rem(other, tm_count)), device_id_type=MESH
        )
        return carry

    lax.fori_loop(1, devices, greet, 0)

    def reach(g):
        @pl.when(tm < tm_count - 1)
        def _():
            early(g).start()

        @pl.when(tm > 0)
        def _():
            late(g).start()

    def prepare(g):
        sub = lax.broadcasted_iota(jnp.int32, (8, LANES), 0)
        for half in range(0, GROUP, 8):
            delay = by_station(delay_ref, g * GROUP, sub + half, (8, LANES))
            lag[half : half + 8, :] = delay
            for tap in range(P_SIZE):
                line = [
                    jnp.broadcast_to(taps_ref[tap : tap + 1, i * LANES : (i + 1) * LANES], (8, LANES))
                    for i in range(tiles)
                ]
                line = roll_left(line, jnp.bitwise_and(delay, C - 1))
                for i in range(tiles):
                    taps[EARLY + tap, half : half + 8, i * LANES : (i + 1) * LANES] = line[i]
        lane = lax.broadcasted_iota(jnp.int32, (8, LANES), 1)
        which = jnp.bitwise_and(lane, GROUP - 1)
        start = by_station(fringe_ref, g * GROUP, which, (8, LANES)) - jnp.where(lane < GROUP, 0, Q // 4)
        rate = by_station(rate_ref, g * GROUP, which, (8, LANES)) - (Q // C) * by_station(
            delay_ref, g * GROUP, which, (8, LANES)
        )

        def angle(block, carry):
            first = pl.multiple_of(block * 32, 32)
            for more in range(0, 32, 8):
                phase_index = jnp.bitwise_and(start + rate * (sub + first + more), Q - 1)
                turn[pl.ds(first + more, 8), :] = jnp.cos(phase_index.astype(jnp.float32) * (TWO_PI / Q)) * (
                    1.0 / math.sqrt(C)
                )
            return carry

        lax.fori_loop(0, C // 32, angle, 0)

    for edge in list(range(EARLY)) + list(range(EARLY + P_SIZE, 2 * EARLY + P_SIZE)):
        taps[edge] = jnp.zeros((GROUP, C), jnp.float32)

    @pl.when(tm == 0)
    def _():
        x[:, :, :, 0 : EARLY * C] = jnp.zeros((groups, 2, GROUP, EARLY * C), x.dtype)

    @pl.when(tm == tm_count - 1)
    def _():
        for g in range(groups):
            x[g, :, :, EARLY * C + samples :] = jnp.zeros((2, GROUP, LATE * C), x.dtype)

    prepare(0)
    pl.semaphore_wait(barrier, devices - 1)
    reach(0)

    def one_group(g, carry):
        load(g).wait()

        @pl.when(tm > 0)
        def _():
            early(g).wait_recv()

        def weigh(low, high, index, carry):
            part = index // tiles
            offset = pl.multiple_of(lax.rem(index, tiles) * LANES, LANES)
            lane = offset + lax.broadcasted_iota(jnp.int32, (8, LANES), 1)
            for half in range(0, GROUP, 8):
                delay = lag[half : half + 8, :]
                behind = lax.shift_right_logical(delay, C.bit_length() - 1) + jnp.where(
                    lane >= C - jnp.bitwise_and(delay, C - 1), 1, 0
                )
                rolled = [taps[q, half : half + 8, pl.ds(offset, LANES)] for q in range(WIDE + EARLY)]
                factor = []
                for q in range(WIDE):
                    value = rolled[q]
                    for back in range(1, EARLY + 1):
                        value = jnp.where(behind == back, rolled[q + back], value)
                    factor.append(value)
                for base in range(low, high, STEP):
                    frames = [
                        x[g, part, :, pl.ds(pl.multiple_of((base + j) * C + offset, LANES), LANES)].astype(
                            jnp.float32
                        )[half : half + 8]
                        for j in range(STEP + WIDE - 1)
                    ]
                    for m in range(STEP):
                        total = factor[0] * frames[m]
                        for q in range(1, WIDE):
                            total = total + factor[q] * frames[m + q]
                        mixed[pl.ds(half * apart + base + m, 8, stride=apart), :] = total
            sign = jnp.where(part == 0, -1.0, 1.0)
            same = pl.multiple_of(part * C + offset, LANES)
            cross = pl.multiple_of((1 - part) * C + offset, LANES)
            for s in range(GROUP):
                value = mixed[s * apart + low : s * apart + high, :]
                first = s * 2 * spectra
                rows[first + low : first + high, pl.ds(same, LANES)] = value.astype(jnp.bfloat16)
                rows[first + spectra + low : first + spectra + high, pl.ds(cross, LANES)] = (value * sign).astype(jnp.bfloat16)
            return carry

        inner = max(0, (spectra - LATE) // 16 * 16)
        if inner:
            lax.fori_loop(0, 2 * tiles, functools.partial(weigh, 0, inner), 0)

        @pl.when(tm < tm_count - 1)
        def _():
            late(g).wait_recv()

        lax.fori_loop(0, 2 * tiles, functools.partial(weigh, inner, spectra), 0)

        @pl.when(g == 0)
        def _():
            whole_table.wait()

        @pl.when(g + 1 < groups)
        def _():
            reach(g + 1)

        def one_chunk(index, carry):
            near = lax.rem(index, 2)
            away = (1 - near) * (chunks // 2) + index // 2
            chunk = jnp.bitwise_xor(me // per_chunk, away)
            first = pl.multiple_of(chunk * CHUNK, CHUNK)
            left = table[pl.ds(first, CHUNK), :]
            width = 2 * spectra
            side = jnp.where(lax.broadcasted_iota(jnp.int32, (CHUNK, width), 1) < spectra, -1.0, 1.0)
            for s in range(0, GROUP, 2):
                product = lax.dot_general(
                    left, rows[s * width : (s + 2) * width, :], (((1,), (1,)), ((), ())),
                    preferred_element_type=jnp.float32,
                )
                for station in (s, s + 1):
                    value = product[:, (station - s) * width : (station - s + 1) * width]
                    cosine = turn[pl.ds(first, CHUNK), station : station + 1]
                    sine = turn[pl.ds(first, CHUNK), GROUP + station : GROUP + station + 1]
                    turned = value * cosine + pltpu.roll(value, spectra, 1) * (side * sine)
                    for c in range(0, CHUNK, 8):
                        flat[pl.ds(c * GROUP + station, 8, stride=GROUP), :] = turned[c : c + 8]

            def pack(block, carry):
                value = flat[pl.ds(pl.multiple_of(block * 128, 128), 128), :].astype(jnp.bfloat16)
                send[g, pl.ds(first + block * (128 // GROUP), 128 // GROUP)] = value.reshape(
                    128 // GROUP, GROUP, width
                )
                return carry

            lax.fori_loop(0, CHUNK * GROUP // 128, pack, 0)

            def go(i, carry):
                mask = away * per_chunk + i

                @pl.when(jnp.logical_and(near == 1, g > 0))
                def _():
                    spread(g, (away + chunks // 2) * per_chunk + i).start()

                @pl.when(jnp.logical_and(mask > 0, jnp.logical_or(near == 1, g == 0)))
                def _():
                    spread(g, mask).start()

                @pl.when(mask == 0)
                def _():
                    keep(g).start()

                return carry

            lax.fori_loop(0, per_chunk, go, 0)
            return carry

        lax.fori_loop(0, chunks, one_chunk, 0)

        @pl.when(g + 1 < groups)
        def _():
            prepare(g + 1)

        return carry

    lax.fori_loop(0, groups, one_group, 0)

    for g in range(groups):
        keep(g).wait()

        def come(mask, carry):
            spread(g, mask).wait()
            return carry

        lax.fori_loop(1, devices, come, 0)

    @pl.when(tm > 0)
    def _():
        for g in range(groups):
            late(g).wait_send()

    @pl.when(tm < tm_count - 1)
    def _():
        for g in range(groups):
            early(g).wait_send()


def spread_spectra(voltages, delays, fringe, fringe_rate, filter_taps, stn_count, tm_count):
    stations, samples = voltages.shape[1:]
    spectra = samples // C
    groups = stations // GROUP
    devices = stn_count * tm_count
    each = C // devices
    width = 2 * spectra
    vmem = pl.BlockSpec(memory_space=pltpu.VMEM)
    smem = pl.BlockSpec(memory_space=pltpu.SMEM)
    hbm = pl.BlockSpec(memory_space=pl.ANY)
    return pl.pallas_call(
        functools.partial(spread_kernel, stn_count, tm_count),
        in_specs=[hbm, hbm, smem, smem, smem, vmem],
        out_specs=hbm,
        out_shape=jax.ShapeDtypeStruct((stn_count, tm_count, groups, each, GROUP, width), jnp.bfloat16),
        scratch_shapes=[
            pltpu.VMEM((groups, 2, GROUP, (EARLY + LATE) * C + samples), jnp.bfloat16),
            pltpu.VMEM((C, 2 * C), jnp.bfloat16),
            pltpu.VMEM((P_SIZE + 2 * EARLY, GROUP, C), jnp.float32),
            pltpu.VMEM((GROUP, LANES), jnp.int32),
            pltpu.VMEM((C, LANES), jnp.float32),
            pltpu.VMEM((GROUP * (spectra + 8), LANES), jnp.float32),
            pltpu.VMEM((GROUP * width, 2 * C), jnp.bfloat16),
            pltpu.VMEM((CHUNK * GROUP, width), jnp.float32),
            pltpu.VMEM((groups, C, GROUP, width), jnp.bfloat16),
            pltpu.SemaphoreType.DMA((groups,)),
            pltpu.SemaphoreType.DMA,
            pltpu.SemaphoreType.DMA((2, groups)),
            pltpu.SemaphoreType.DMA((2, groups)),
            pltpu.SemaphoreType.DMA((groups, devices)),
            pltpu.SemaphoreType.DMA((groups, devices)),
            pltpu.SemaphoreType.DMA((groups,)),
        ],
        compiler_params=pltpu.CompilerParams(
            collective_id=0, has_side_effects=True, vmem_limit_bytes=60 * 1024 * 1024
        ),
    )(voltages, jnp.asarray(dft_table()), delays, fringe, fringe_rate, filter_taps)


def gram_kernel(scale, spectra_ref, real_ref, imag_ref):
    stn_count, tm_count, groups, channels, size, width = spectra_ref.shape
    whole = stn_count * groups * size
    lane = lax.broadcasted_iota(jnp.int32, (whole, width), 1)
    last = (((1,), (1,)), ((), ()))
    for channel in range(channels):
        pieces, turned_pieces = [], []
        for source in range(tm_count):
            piece = spectra_ref[:, source, :, channel].reshape(whole, width)
            turned = pltpu.roll(piece.astype(jnp.float32), width // 2, 1)
            pieces.append(piece)
            turned_pieces.append(jnp.where(lane < width // 2, turned, -turned).astype(jnp.bfloat16))
        rows = jnp.concatenate(pieces, axis=1)
        swapped = jnp.concatenate(turned_pieces, axis=1)
        real_ref[channel] = lax.dot_general(rows, rows, last, preferred_element_type=jnp.float32) * scale
        imag_ref[channel] = lax.dot_general(swapped, rows, last, preferred_element_type=jnp.float32) * scale


def grams(received, scale):
    stn_count, tm_count, groups, channels, size, width = received.shape
    whole = stn_count * groups * size
    step = 2
    result = jax.ShapeDtypeStruct((channels, whole, whole), jnp.float32)
    return pl.pallas_call(
        functools.partial(gram_kernel, scale),
        grid=(channels // step,),
        in_specs=[pl.BlockSpec((stn_count, tm_count, groups, step, size, width), lambda c: (0, 0, 0, c, 0, 0))],
        out_specs=[pl.BlockSpec((step, whole, whole), lambda c: (c, 0, 0))] * 2,
        out_shape=[result, result],
        compiler_params=pltpu.CompilerParams(vmem_limit_bytes=60 * 1024 * 1024),
    )(received)


def local(stn_count, tm_count, voltages, delays, fringe, fringe_rate, filter_taps):
    spectra = voltages.shape[2] // C
    received = spread_spectra(voltages, delays, fringe, fringe_rate, filter_taps, stn_count, tm_count)
    real, imag = grams(received, 1.0 / (spectra * tm_count))
    return (real, imag)


def solution(mesh):
    return jax.shard_map(
        functools.partial(local, mesh.shape["stn"], mesh.shape["tm"]),
        mesh=mesh,
        in_specs=(P(None, "stn", "tm"), P("stn"), P("stn"), P("stn"), P()),
        out_specs=(P(("stn", "tm"), None, None), P(("stn", "tm"), None, None)),
        check_vma=False,
    )
```

```python
import functools
import math

import jax
import jax.numpy as jnp
import numpy as np
from jax import lax
from jax.experimental import pallas as pl
from jax.experimental.pallas import tpu as pltpu
from jax.sharding import PartitionSpec as P

C = 1024
P_SIZE = 16
Q = 4096
DMAX = 2048

TWO_PI = 2.0 * math.pi
LANES = 128
GROUP = 16
CHUNK = 256
STEP = 16
PEERS = 4
TAIL = 4
EARLY = DMAX // C
LATE = P_SIZE - 1
WIDE = P_SIZE + EARLY
MESH = pl.DeviceIdType.MESH


def dft_table():
    column = np.arange(C, dtype=np.int64)
    angles = (column[:, None] * column[None, :] % C).astype(np.float32) * np.float32(TWO_PI / C)
    both = np.concatenate([np.cos(angles), np.sin(angles)], axis=1)
    return both.astype(jnp.bfloat16)


def roll_left(tiles, amount):
    count = len(tiles)
    lane = lax.broadcasted_iota(jnp.int32, tiles[0].shape, 1)
    within = jnp.bitwise_and(amount, LANES - 1)
    source = jnp.bitwise_and(lane + within, LANES - 1)
    turned = [jnp.take_along_axis(tile, source, axis=1) for tile in tiles]
    line = [jnp.where(lane < LANES - within, turned[i], turned[(i + 1) % count]) for i in range(count)]
    step = 1
    while step < count:
        chosen = jnp.bitwise_and(amount, step * LANES) != 0
        line = [jnp.where(chosen, line[(i + step) % count], line[i]) for i in range(count)]
        step *= 2
    return line


def by_station(ref, first, index, shape):
    value = jnp.zeros(shape, jnp.int32)
    for i in range(GROUP):
        value = jnp.where(index == i, ref[first + i], value)
    return value


def spread_kernel(
    stn_count, tm_count, volt, table_ref, delay_ref, fringe_ref, rate_ref, taps_ref, recv, *rest
):
    tails = rest[:PEERS]
    (
        x, table, taps, lag, turn, mixed, rows, flat, send,
        load_sem, table_sem, early_sems, late_sems, send_sems, recv_sems, own_sems, tail_sems,
    ) = rest[PEERS:]
    stn, tm = lax.axis_index("stn"), lax.axis_index("tm")
    me = stn * tm_count + tm
    devices = stn_count * tm_count
    groups = x.shape[0]
    samples = volt.shape[2]
    spectra = samples // C
    each = C // devices
    per_chunk = CHUNK // each
    chunks = C // CHUNK
    tiles = C // LANES
    apart = mixed.shape[0] // GROUP
    later = tails[0].shape[1]
    opposite = devices // 2

    def load(g):
        return pltpu.make_async_copy(
            volt.at[:, pl.ds(g * GROUP, GROUP), :],
            x.at[g, :, :, pl.ds(EARLY * C, samples)],
            load_sem.at[g],
        )

    def early(g):
        return pltpu.make_async_remote_copy(
            volt.at[:, pl.ds(g * GROUP, GROUP), pl.ds(samples - EARLY * C, EARLY * C)],
            x.at[g, :, :, pl.ds(0, EARLY * C)],
            early_sems.at[0, g], early_sems.at[1, g],
            device_id=(stn, lax.rem(tm + 1, tm_count)), device_id_type=MESH,
        )

    def late(g):
        return pltpu.make_async_remote_copy(
            volt.at[:, pl.ds(g * GROUP, GROUP), pl.ds(0, LATE * C)],
            x.at[g, :, :, pl.ds(EARLY * C + samples, LATE * C)],
            late_sems.at[0, g], late_sems.at[1, g],
            device_id=(stn, lax.rem(tm + tm_count - 1, tm_count)), device_id_type=MESH,
        )

    def spread(g, mask):
        other = jnp.bitwise_xor(me, mask)
        return pltpu.make_async_remote_copy(
            send.at[g, pl.ds(other * each, each)],
            recv.at[stn, tm, g],
            send_sems.at[g, mask], recv_sems.at[g, mask],
            device_id=(other // tm_count, lax.rem(other, tm_count)), device_id_type=MESH,
        )

    def spread_part(g, mask):
        other = jnp.bitwise_xor(me, mask)
        return pltpu.make_async_remote_copy(
            send.at[g, pl.ds(other * each, each - later)],
            recv.at[stn, tm, g, pl.ds(0, each - later)],
            send_sems.at[g, mask], recv_sems.at[g, mask],
            device_id=(other // tm_count, lax.rem(other, tm_count)), device_id_type=MESH,
        )

    def both(mask, act, g):
        partly = jnp.logical_and(mask >= opposite, mask < opposite + PEERS)

        @pl.when(partly)
        def _():
            act(spread_part(g, mask))

        @pl.when(jnp.logical_not(partly))
        def _():
            act(spread(g, mask))

    def tail(g, k):
        other = jnp.bitwise_xor(me, opposite + k)
        return pltpu.make_async_copy(
            send.at[g, pl.ds(other * each + each - later, later)], tails[k].at[g], tail_sems.at[k, g]
        )

    def keep(g):
        return pltpu.make_async_copy(send.at[g, pl.ds(me * each, each)], recv.at[stn, tm, g], own_sems.at[g])

    whole_table = pltpu.make_async_copy(table_ref, table, table_sem)
    load(0).start()
    whole_table.start()
    for g in range(1, groups):
        load(g).start()

    barrier = pltpu.get_barrier_semaphore()

    def greet(mask, carry):
        other = jnp.bitwise_xor(me, mask)
        pl.semaphore_signal(
            barrier, inc=1, device_id=(other // tm_count, lax.rem(other, tm_count)), device_id_type=MESH
        )
        return carry

    lax.fori_loop(1, devices, greet, 0)

    def reach(g):
        @pl.when(tm < tm_count - 1)
        def _():
            early(g).start()

        @pl.when(tm > 0)
        def _():
            late(g).start()

    def prepare(g):
        sub = lax.broadcasted_iota(jnp.int32, (8, LANES), 0)
        for half in range(0, GROUP, 8):
            delay = by_station(delay_ref, g * GROUP, sub + half, (8, LANES))
            lag[half : half + 8, :] = delay
            for tap in range(P_SIZE):
                line = [
                    jnp.broadcast_to(taps_ref[tap : tap + 1, i * LANES : (i + 1) * LANES], (8, LANES))
                    for i in range(tiles)
                ]
                line = roll_left(line, jnp.bitwise_and(delay, C - 1))
                for i in range(tiles):
                    taps[EARLY + tap, half : half + 8, i * LANES : (i + 1) * LANES] = line[i]
        lane = lax.broadcasted_iota(jnp.int32, (8, LANES), 1)
        which = jnp.bitwise_and(lane, GROUP - 1)
        start = by_station(fringe_ref, g * GROUP, which, (8, LANES)) - jnp.where(lane < GROUP, 0, Q // 4)
        rate = by_station(rate_ref, g * GROUP, which, (8, LANES)) - (Q // C) * by_station(
            delay_ref, g * GROUP, which, (8, LANES)
        )

        def angle(block, carry):
            first = pl.multiple_of(block * 32, 32)
            for more in range(0, 32, 8):
                phase_index = jnp.bitwise_and(start + rate * (sub + first + more), Q - 1)
                turn[pl.ds(first + more, 8), :] = jnp.cos(phase_index.astype(jnp.float32) * (TWO_PI / Q)) * (
                    1.0 / math.sqrt(C)
                )
            return carry

        lax.fori_loop(0, C // 32, angle, 0)

    for edge in list(range(EARLY)) + list(range(EARLY + P_SIZE, 2 * EARLY + P_SIZE)):
        taps[edge] = jnp.zeros((GROUP, C), jnp.float32)

    @pl.when(tm == 0)
    def _():
        x[:, :, :, 0 : EARLY * C] = jnp.zeros((groups, 2, GROUP, EARLY * C), x.dtype)

    @pl.when(tm == tm_count - 1)
    def _():
        for g in range(groups):
            x[g, :, :, EARLY * C + samples :] = jnp.zeros((2, GROUP, LATE * C), x.dtype)

    prepare(0)
    pl.semaphore_wait(barrier, devices - 1)
    reach(0)

    def one_group(g, carry):
        load(g).wait()

        @pl.when(tm > 0)
        def _():
            early(g).wait_recv()

        def weigh(low, high, index, carry):
            part = index // tiles
            offset = pl.multiple_of(lax.rem(index, tiles) * LANES, LANES)
            lane = offset + lax.broadcasted_iota(jnp.int32, (8, LANES), 1)
            for half in range(0, GROUP, 8):
                delay = lag[half : half + 8, :]
                behind = lax.shift_right_logical(delay, C.bit_length() - 1) + jnp.where(
                    lane >= C - jnp.bitwise_and(delay, C - 1), 1, 0
                )
                rolled = [taps[q, half : half + 8, pl.ds(offset, LANES)] for q in range(WIDE + EARLY)]
                factor = []
                for q in range(WIDE):
                    value = rolled[q]
                    for back in range(1, EARLY + 1):
                        value = jnp.where(behind == back, rolled[q + back], value)
                    factor.append(value)
                for base in range(low, high, STEP):
                    frames = [
                        x[g, part, :, pl.ds(pl.multiple_of((base + j) * C + offset, LANES), LANES)].astype(
                            jnp.float32
                        )[half : half + 8]
                        for j in range(STEP + WIDE - 1)
                    ]
                    for m in range(STEP):
                        total = factor[0] * frames[m]
                        for q in range(1, WIDE):
                            total = total + factor[q] * frames[m + q]
                        mixed[pl.ds(half * apart + base + m, 8, stride=apart), :] = total
            sign = jnp.where(part == 0, -1.0, 1.0)
            same = pl.multiple_of(part * C + offset, LANES)
            cross = pl.multiple_of((1 - part) * C + offset, LANES)
            for s in range(GROUP):
                value = mixed[s * apart + low : s * apart + high, :]
                first = s * 2 * spectra
                rows[first + low : first + high, pl.ds(same, LANES)] = value.astype(jnp.bfloat16)
                rows[first + spectra + low : first + spectra + high, pl.ds(cross, LANES)] = (value * sign).astype(jnp.bfloat16)
            return carry

        inner = max(0, (spectra - LATE) // 16 * 16)
        if inner:
            lax.fori_loop(0, 2 * tiles, functools.partial(weigh, 0, inner), 0)

        @pl.when(tm < tm_count - 1)
        def _():
            late(g).wait_recv()

        lax.fori_loop(0, 2 * tiles, functools.partial(weigh, inner, spectra), 0)

        @pl.when(g == 0)
        def _():
            whole_table.wait()

        @pl.when(g + 1 < groups)
        def _():
            reach(g + 1)

        def one_chunk(index, carry):
            near = lax.rem(index, 2)
            away = (1 - near) * (chunks // 2) + index // 2
            chunk = jnp.bitwise_xor(me // per_chunk, away)
            first = pl.multiple_of(chunk * CHUNK, CHUNK)
            left = table[pl.ds(first, CHUNK), :]
            width = 2 * spectra
            side = jnp.where(lax.broadcasted_iota(jnp.int32, (CHUNK, width), 1) < spectra, -1.0, 1.0)
            for s in range(0, GROUP, 2):
                product = lax.dot_general(
                    left, rows[s * width : (s + 2) * width, :], (((1,), (1,)), ((), ())),
                    preferred_element_type=jnp.float32,
                )
                for station in (s, s + 1):
                    value = product[:, (station - s) * width : (station - s + 1) * width]
                    cosine = turn[pl.ds(first, CHUNK), station : station + 1]
                    sine = turn[pl.ds(first, CHUNK), GROUP + station : GROUP + station + 1]
                    turned = value * cosine + pltpu.roll(value, spectra, 1) * (side * sine)
                    for c in range(0, CHUNK, 8):
                        flat[pl.ds(c * GROUP + station, 8, stride=GROUP), :] = turned[c : c + 8]

            def pack(block, carry):
                value = flat[pl.ds(pl.multiple_of(block * 128, 128), 128), :].astype(jnp.bfloat16)
                send[g, pl.ds(first + block * (128 // GROUP), 128 // GROUP)] = value.reshape(
                    128 // GROUP, GROUP, width
                )
                return carry

            lax.fori_loop(0, CHUNK * GROUP // 128, pack, 0)

            @pl.when(index == 0)
            def _():
                for k in range(PEERS):
                    tail(g, k).start()

            def go(i, carry):
                mask = away * per_chunk + i

                @pl.when(jnp.logical_and(near == 1, g > 0))
                def _():
                    both((away + chunks // 2) * per_chunk + i, lambda copy: copy.start(), g)

                @pl.when(jnp.logical_and(mask > 0, jnp.logical_or(near == 1, g == 0)))
                def _():
                    both(mask, lambda copy: copy.start(), g)

                @pl.when(mask == 0)
                def _():
                    keep(g).start()

                return carry

            lax.fori_loop(0, per_chunk, go, 0)
            return carry

        lax.fori_loop(0, chunks, one_chunk, 0)

        @pl.when(g + 1 < groups)
        def _():
            prepare(g + 1)

        return carry

    lax.fori_loop(0, groups, one_group, 0)

    for g in range(groups):
        keep(g).wait()
        for k in range(PEERS):
            tail(g, k).wait()

        def come(mask, carry):
            both(mask, lambda copy: copy.wait(), g)
            return carry

        lax.fori_loop(1, devices, come, 0)

    @pl.when(tm > 0)
    def _():
        for g in range(groups):
            late(g).wait_send()

    @pl.when(tm < tm_count - 1)
    def _():
        for g in range(groups):
            early(g).wait_send()


def spread_spectra(voltages, delays, fringe, fringe_rate, filter_taps, stn_count, tm_count):
    stations, samples = voltages.shape[1:]
    spectra = samples // C
    groups = stations // GROUP
    devices = stn_count * tm_count
    each = C // devices
    width = 2 * spectra
    later = each // TAIL
    vmem = pl.BlockSpec(memory_space=pltpu.VMEM)
    smem = pl.BlockSpec(memory_space=pltpu.SMEM)
    hbm = pl.BlockSpec(memory_space=pl.ANY)
    return pl.pallas_call(
        functools.partial(spread_kernel, stn_count, tm_count),
        in_specs=[hbm, hbm, smem, smem, smem, vmem],
        out_specs=[hbm] * (1 + PEERS),
        out_shape=[jax.ShapeDtypeStruct((stn_count, tm_count, groups, each, GROUP, width), jnp.bfloat16)]
        + [jax.ShapeDtypeStruct((groups, later, GROUP, width), jnp.bfloat16)] * PEERS,
        scratch_shapes=[
            pltpu.VMEM((groups, 2, GROUP, (EARLY + LATE) * C + samples), jnp.bfloat16),
            pltpu.VMEM((C, 2 * C), jnp.bfloat16),
            pltpu.VMEM((P_SIZE + 2 * EARLY, GROUP, C), jnp.float32),
            pltpu.VMEM((GROUP, LANES), jnp.int32),
            pltpu.VMEM((C, LANES), jnp.float32),
            pltpu.VMEM((GROUP * (spectra + 8), LANES), jnp.float32),
            pltpu.VMEM((GROUP * width, 2 * C), jnp.bfloat16),
            pltpu.VMEM((CHUNK * GROUP, width), jnp.float32),
            pltpu.VMEM((groups, C, GROUP, width), jnp.bfloat16),
            pltpu.SemaphoreType.DMA((groups,)),
            pltpu.SemaphoreType.DMA,
            pltpu.SemaphoreType.DMA((2, groups)),
            pltpu.SemaphoreType.DMA((2, groups)),
            pltpu.SemaphoreType.DMA((groups, devices)),
            pltpu.SemaphoreType.DMA((groups, devices)),
            pltpu.SemaphoreType.DMA((groups,)),
            pltpu.SemaphoreType.DMA((PEERS, groups)),
        ],
        compiler_params=pltpu.CompilerParams(
            collective_id=0, has_side_effects=True, vmem_limit_bytes=60 * 1024 * 1024
        ),
    )(voltages, jnp.asarray(dft_table()), delays, fringe, fringe_rate, filter_taps)


def gram_kernel(scale, late_count, spectra_ref, *refs):
    stn_count, tm_count, groups, channels, size, width = spectra_ref.shape
    if late_count:
        real_ref, imag_ref, filled = refs[late_count + 2 :]
        stn, tm = lax.axis_index("stn"), lax.axis_index("tm")
        filled[...] = spectra_ref[...]
        for k in range(late_count):
            filled[jnp.bitwise_xor(stn, stn_count // 2), jnp.bitwise_xor(tm, k)] = refs[k][...]
    else:
        real_ref, imag_ref = refs
        filled = spectra_ref
    whole = stn_count * groups * size
    lane = lax.broadcasted_iota(jnp.int32, (whole, width), 1)
    last = (((1,), (1,)), ((), ()))
    for channel in range(channels):
        pieces, turned_pieces = [], []
        for source in range(tm_count):
            piece = filled[:, source, :, channel].reshape(whole, width)
            turned = pltpu.roll(piece.astype(jnp.float32), width // 2, 1)
            pieces.append(piece)
            turned_pieces.append(jnp.where(lane < width // 2, turned, -turned).astype(jnp.bfloat16))
        rows = jnp.concatenate(pieces, axis=1)
        swapped = jnp.concatenate(turned_pieces, axis=1)
        real_ref[channel] = lax.dot_general(rows, rows, last, preferred_element_type=jnp.float32) * scale
        imag_ref[channel] = lax.dot_general(swapped, rows, last, preferred_element_type=jnp.float32) * scale


def grams(received, scale, first, count, late=(), begun=()):
    stn_count, tm_count, groups, channels, size, width = received.shape
    whole = stn_count * groups * size
    step = 2
    base = first // step
    block = (stn_count, tm_count, groups, step, size, width)
    result = jax.ShapeDtypeStruct((channels, whole, whole), jnp.float32)
    inner = tm_count * width
    return pl.pallas_call(
        functools.partial(gram_kernel, scale, len(late)),
        grid=(count // step,),
        in_specs=[pl.BlockSpec(block, lambda c: (0, 0, 0, base + c, 0, 0))]
        + [pl.BlockSpec((groups, step, size, width), lambda c: (0, c, 0, 0))] * len(late)
        + [pl.BlockSpec(memory_space=pl.ANY)] * len(begun),
        out_specs=[pl.BlockSpec((step, whole, whole), lambda c: (base + c, 0, 0))] * 2,
        out_shape=[result, result],
        scratch_shapes=[pltpu.VMEM(block, received.dtype)] if late else [],
        input_output_aliases={1 + len(late) + i: i for i in range(len(begun))},
        compiler_params=pltpu.CompilerParams(vmem_limit_bytes=60 * 1024 * 1024),
        cost_estimate=pl.CostEstimate(
            flops=4 * count * whole * whole * inner,
            bytes_accessed=count * whole * (8 * whole + 2 * inner),
            transcendentals=0,
        ),
    )(received, *late, *begun)


def local(stn_count, tm_count, voltages, delays, fringe, fringe_rate, filter_taps):
    spectra = voltages.shape[2] // C
    devices = stn_count * tm_count
    received, *tails = spread_spectra(voltages, delays, fringe, fringe_rate, filter_taps, stn_count, tm_count)
    late = [
        lax.ppermute(tail, ("stn", "tm"), [(i, i ^ (devices // 2 + k)) for i in range(devices)])
        for k, tail in enumerate(tails)
    ]
    scale = 1.0 / (spectra * tm_count)
    channels, later = received.shape[3], tails[0].shape[1]
    begun = grams(received, scale, 0, channels - later)
    real, imag = grams(received, scale, channels - later, later, late, begun)
    return (real, imag)


def solution(mesh):
    return jax.shard_map(
        functools.partial(local, mesh.shape["stn"], mesh.shape["tm"]),
        mesh=mesh,
        in_specs=(P(None, "stn", "tm"), P("stn"), P("stn"), P("stn"), P()),
        out_specs=(P(("stn", "tm"), None, None), P(("stn", "tm"), None, None)),
        check_vma=False,
    )
```

```python
import functools
import math

import jax
import jax.numpy as jnp
import numpy as np
from jax import lax
from jax.experimental import pallas as pl
from jax.experimental.pallas import tpu as pltpu
from jax.sharding import PartitionSpec as P

C = 1024
P_SIZE = 16
Q = 4096
DMAX = 2048

TWO_PI = 2.0 * math.pi
LANES = 128
GROUP = 16
PART = 8
PAIR = GROUP // PART
CHUNK = 256
STEP = 16
PEERS = 4
TAIL = 4
EARLY = DMAX // C
LATE = P_SIZE - 1
WIDE = P_SIZE + EARLY
MESH = pl.DeviceIdType.MESH


def dft_table():
    column = np.arange(C, dtype=np.int64)
    angles = (column[:, None] * column[None, :] % C).astype(np.float32) * np.float32(TWO_PI / C)
    both = np.concatenate([np.cos(angles), np.sin(angles)], axis=1)
    return both.astype(jnp.bfloat16)


def roll_left(tiles, amount):
    count = len(tiles)
    lane = lax.broadcasted_iota(jnp.int32, tiles[0].shape, 1)
    within = jnp.bitwise_and(amount, LANES - 1)
    source = jnp.bitwise_and(lane + within, LANES - 1)
    turned = [jnp.take_along_axis(tile, source, axis=1) for tile in tiles]
    line = [jnp.where(lane < LANES - within, turned[i], turned[(i + 1) % count]) for i in range(count)]
    step = 1
    while step < count:
        chosen = jnp.bitwise_and(amount, step * LANES) != 0
        line = [jnp.where(chosen, line[(i + step) % count], line[i]) for i in range(count)]
        step *= 2
    return line


def by_station(ref, first, index, shape):
    value = jnp.zeros(shape, jnp.int32)
    for i in range(PART):
        value = jnp.where(index == i, ref[first + i], value)
    return value


def spread_kernel(
    stn_count, tm_count, volt, table_ref, delay_ref, fringe_ref, rate_ref, taps_ref, recv, *rest
):
    tails = rest[:PEERS]
    (
        x, table, taps, lag, turn, mixed, rows, flat, send,
        load_sem, table_sem, early_sems, late_sems, send_sems, recv_sems, own_sems, tail_sems,
    ) = rest[PEERS:]
    stn, tm = lax.axis_index("stn"), lax.axis_index("tm")
    me = stn * tm_count + tm
    devices = stn_count * tm_count
    groups, steps = x.shape[0], send.shape[0]
    samples = volt.shape[2]
    spectra = samples // C
    each = C // devices
    per_chunk = CHUNK // each
    packed = each // PAIR
    chunks = C // CHUNK
    tiles = C // LANES
    apart = mixed.shape[0] // PART
    later = tails[0].shape[1]
    opposite = devices // 2

    def load(g):
        return pltpu.make_async_copy(
            volt.at[:, pl.ds(g * GROUP, GROUP), :],
            x.at[g, :, :, pl.ds(EARLY * C, samples)],
            load_sem.at[g],
        )

    def early(g):
        return pltpu.make_async_remote_copy(
            volt.at[:, pl.ds(g * GROUP, GROUP), pl.ds(samples - EARLY * C, EARLY * C)],
            x.at[g, :, :, pl.ds(0, EARLY * C)],
            early_sems.at[0, g], early_sems.at[1, g],
            device_id=(stn, lax.rem(tm + 1, tm_count)), device_id_type=MESH,
        )

    def late(g):
        return pltpu.make_async_remote_copy(
            volt.at[:, pl.ds(g * GROUP, GROUP), pl.ds(0, LATE * C)],
            x.at[g, :, :, pl.ds(EARLY * C + samples, LATE * C)],
            late_sems.at[0, g], late_sems.at[1, g],
            device_id=(stn, lax.rem(tm + tm_count - 1, tm_count)), device_id_type=MESH,
        )

    def spread(g, mask):
        other = jnp.bitwise_xor(me, mask)
        return pltpu.make_async_remote_copy(
            send.at[g, pl.ds(other * packed, packed)],
            recv.at[stn, tm, g],
            send_sems.at[g, mask], recv_sems.at[g, mask],
            device_id=(other // tm_count, lax.rem(other, tm_count)), device_id_type=MESH,
        )

    def spread_part(g, mask):
        other = jnp.bitwise_xor(me, mask)
        return pltpu.make_async_remote_copy(
            send.at[g, pl.ds(other * packed, packed - later)],
            recv.at[stn, tm, g, pl.ds(0, packed - later)],
            send_sems.at[g, mask], recv_sems.at[g, mask],
            device_id=(other // tm_count, lax.rem(other, tm_count)), device_id_type=MESH,
        )

    def both(mask, act, g):
        partly = jnp.logical_and(mask >= opposite, mask < opposite + PEERS)

        @pl.when(partly)
        def _():
            act(spread_part(g, mask))

        @pl.when(jnp.logical_not(partly))
        def _():
            act(spread(g, mask))

    def tail(g, k):
        other = jnp.bitwise_xor(me, opposite + k)
        return pltpu.make_async_copy(
            send.at[g, pl.ds(other * packed + packed - later, later)], tails[k].at[g], tail_sems.at[k, g]
        )

    def keep(g):
        return pltpu.make_async_copy(send.at[g, pl.ds(me * packed, packed)], recv.at[stn, tm, g], own_sems.at[g])

    whole_table = pltpu.make_async_copy(table_ref, table, table_sem)
    load(0).start()
    whole_table.start()
    for g in range(1, groups):
        load(g).start()

    barrier = pltpu.get_barrier_semaphore()

    def greet(mask, carry):
        other = jnp.bitwise_xor(me, mask)
        pl.semaphore_signal(
            barrier, inc=1, device_id=(other // tm_count, lax.rem(other, tm_count)), device_id_type=MESH
        )
        return carry

    lax.fori_loop(1, devices, greet, 0)

    def reach(g):
        @pl.when(tm < tm_count - 1)
        def _():
            early(g).start()

        @pl.when(tm > 0)
        def _():
            late(g).start()

    def prepare(step):
        first_station = step * PART
        sub = lax.broadcasted_iota(jnp.int32, (8, LANES), 0)
        delay = by_station(delay_ref, first_station, sub, (8, LANES))
        lag[...] = delay
        for tap in range(P_SIZE):
            line = [
                jnp.broadcast_to(taps_ref[tap : tap + 1, i * LANES : (i + 1) * LANES], (8, LANES))
                for i in range(tiles)
            ]
            line = roll_left(line, jnp.bitwise_and(delay, C - 1))
            for i in range(tiles):
                taps[EARLY + tap, :, i * LANES : (i + 1) * LANES] = line[i]
        lane = lax.broadcasted_iota(jnp.int32, (8, LANES), 1)
        which = jnp.bitwise_and(lane, PART - 1)
        start = by_station(fringe_ref, first_station, which, (8, LANES)) - jnp.where(lane < PART, 0, Q // 4)
        rate = by_station(rate_ref, first_station, which, (8, LANES)) - (Q // C) * by_station(
            delay_ref, first_station, which, (8, LANES)
        )

        def angle(block, carry):
            first = pl.multiple_of(block * 32, 32)
            for more in range(0, 32, 8):
                phase_index = jnp.bitwise_and(start + rate * (sub + first + more), Q - 1)
                turn[pl.ds(first + more, 8), :] = jnp.cos(phase_index.astype(jnp.float32) * (TWO_PI / Q)) * (
                    1.0 / math.sqrt(C)
                )
            return carry

        lax.fori_loop(0, C // 32, angle, 0)

    for edge in list(range(EARLY)) + list(range(EARLY + P_SIZE, 2 * EARLY + P_SIZE)):
        taps[edge] = jnp.zeros((PART, C), jnp.float32)

    @pl.when(tm == 0)
    def _():
        x[:, :, :, 0 : EARLY * C] = jnp.zeros((groups, 2, GROUP, EARLY * C), x.dtype)

    @pl.when(tm == tm_count - 1)
    def _():
        for g in range(groups):
            x[g, :, :, EARLY * C + samples :] = jnp.zeros((2, GROUP, LATE * C), x.dtype)

    prepare(0)
    pl.semaphore_wait(barrier, devices - 1)
    reach(0)

    def one_step(step, carry):
        g, second = step // PAIR, lax.rem(step, PAIR)

        @pl.when(second == 0)
        def _():
            load(g).wait()

            @pl.when(tm > 0)
            def _():
                early(g).wait_recv()

        def weigh(low, high, index, carry):
            part = index // tiles
            offset = pl.multiple_of(lax.rem(index, tiles) * LANES, LANES)
            lane = offset + lax.broadcasted_iota(jnp.int32, (8, LANES), 1)
            delay = lag[...]
            behind = lax.shift_right_logical(delay, C.bit_length() - 1) + jnp.where(
                lane >= C - jnp.bitwise_and(delay, C - 1), 1, 0
            )
            rolled = [taps[q, :, pl.ds(offset, LANES)] for q in range(WIDE + EARLY)]
            factor = []
            for q in range(WIDE):
                value = rolled[q]
                for back in range(1, EARLY + 1):
                    value = jnp.where(behind == back, rolled[q + back], value)
                factor.append(value)
            for base in range(low, high, STEP):
                frames = []
                for j in range(STEP + WIDE - 1):
                    value = x[
                        g, part, :, pl.ds(pl.multiple_of((base + j) * C + offset, LANES), LANES)
                    ].astype(jnp.float32)
                    frames.append(jnp.where(second == 0, value[:PART], value[PART:]))
                for m in range(STEP):
                    total = factor[0] * frames[m]
                    for q in range(1, WIDE):
                        total = total + factor[q] * frames[m + q]
                    mixed[pl.ds(base + m, 8, stride=apart), :] = total
            sign = jnp.where(part == 0, -1.0, 1.0)
            same = pl.multiple_of(part * C + offset, LANES)
            cross = pl.multiple_of((1 - part) * C + offset, LANES)
            for s in range(PART):
                value = mixed[s * apart + low : s * apart + high, :]
                first = s * 2 * spectra
                rows[first + low : first + high, pl.ds(same, LANES)] = value.astype(jnp.bfloat16)
                rows[first + spectra + low : first + spectra + high, pl.ds(cross, LANES)] = (value * sign).astype(jnp.bfloat16)
            return carry

        inner = max(0, (spectra - LATE) // 16 * 16)
        if inner:
            lax.fori_loop(0, 2 * tiles, functools.partial(weigh, 0, inner), 0)

        @pl.when(jnp.logical_and(second == 0, tm < tm_count - 1))
        def _():
            late(g).wait_recv()

        lax.fori_loop(0, 2 * tiles, functools.partial(weigh, inner, spectra), 0)

        @pl.when(step == 0)
        def _():
            whole_table.wait()

        @pl.when(jnp.logical_and(second == PAIR - 1, g + 1 < groups))
        def _():
            reach(g + 1)

        def one_chunk(index, carry):
            near = lax.rem(index, 2)
            away = (1 - near) * (chunks // 2) + index // 2
            chunk = jnp.bitwise_xor(me // per_chunk, away)
            first = pl.multiple_of(chunk * CHUNK, CHUNK)
            left = table[pl.ds(first, CHUNK), :]
            width = 2 * spectra
            side = jnp.where(lax.broadcasted_iota(jnp.int32, (CHUNK, width), 1) < spectra, -1.0, 1.0)
            for s in range(0, PART, 2):
                product = lax.dot_general(
                    left, rows[s * width : (s + 2) * width, :], (((1,), (1,)), ((), ())),
                    preferred_element_type=jnp.float32,
                )
                for station in (s, s + 1):
                    value = product[:, (station - s) * width : (station - s + 1) * width]
                    cosine = turn[pl.ds(first, CHUNK), station : station + 1]
                    sine = turn[pl.ds(first, CHUNK), PART + station : PART + station + 1]
                    turned = value * cosine + pltpu.roll(value, spectra, 1) * (side * sine)
                    for c in range(0, CHUNK, 8):
                        flat[pl.ds(c * PART + station, 8, stride=PART), :] = turned[c : c + 8]

            def pack(block, carry):
                value = flat[pl.ds(pl.multiple_of(block * 128, 128), 128), :].astype(jnp.bfloat16)
                send[step, pl.ds(first // PAIR + block * (128 // GROUP), 128 // GROUP)] = value.reshape(
                    128 // GROUP, GROUP, width
                )
                return carry

            lax.fori_loop(0, CHUNK * PART // 128, pack, 0)

            @pl.when(index == 0)
            def _():
                for k in range(PEERS):
                    tail(step, k).start()

            def go(i, carry):
                mask = away * per_chunk + i

                @pl.when(jnp.logical_and(near == 1, step > 0))
                def _():
                    both((away + chunks // 2) * per_chunk + i, lambda copy: copy.start(), step)

                @pl.when(jnp.logical_and(mask > 0, jnp.logical_or(near == 1, step == 0)))
                def _():
                    both(mask, lambda copy: copy.start(), step)

                @pl.when(mask == 0)
                def _():
                    keep(step).start()

                return carry

            lax.fori_loop(0, per_chunk, go, 0)
            return carry

        lax.fori_loop(0, chunks, one_chunk, 0)

        @pl.when(step + 1 < steps)
        def _():
            prepare(step + 1)

        return carry

    lax.fori_loop(0, steps, one_step, 0)

    for g in range(steps):
        keep(g).wait()
        for k in range(PEERS):
            tail(g, k).wait()

        def come(mask, carry):
            both(mask, lambda copy: copy.wait(), g)
            return carry

        lax.fori_loop(1, devices, come, 0)

    @pl.when(tm > 0)
    def _():
        for g in range(groups):
            late(g).wait_send()

    @pl.when(tm < tm_count - 1)
    def _():
        for g in range(groups):
            early(g).wait_send()


def spread_spectra(voltages, delays, fringe, fringe_rate, filter_taps, stn_count, tm_count):
    stations, samples = voltages.shape[1:]
    spectra = samples // C
    groups = stations // GROUP
    devices = stn_count * tm_count
    each = C // devices
    width = 2 * spectra
    steps = groups * PAIR
    packed = each // PAIR
    later = packed // TAIL
    vmem = pl.BlockSpec(memory_space=pltpu.VMEM)
    smem = pl.BlockSpec(memory_space=pltpu.SMEM)
    hbm = pl.BlockSpec(memory_space=pl.ANY)
    return pl.pallas_call(
        functools.partial(spread_kernel, stn_count, tm_count),
        in_specs=[hbm, hbm, smem, smem, smem, vmem],
        out_specs=[hbm] * (1 + PEERS),
        out_shape=[jax.ShapeDtypeStruct((stn_count, tm_count, steps, packed, GROUP, width), jnp.bfloat16)]
        + [jax.ShapeDtypeStruct((steps, later, GROUP, width), jnp.bfloat16)] * PEERS,
        scratch_shapes=[
            pltpu.VMEM((groups, 2, GROUP, (EARLY + LATE) * C + samples), jnp.bfloat16),
            pltpu.VMEM((C, 2 * C), jnp.bfloat16),
            pltpu.VMEM((P_SIZE + 2 * EARLY, PART, C), jnp.float32),
            pltpu.VMEM((PART, LANES), jnp.int32),
            pltpu.VMEM((C, LANES), jnp.float32),
            pltpu.VMEM((PART * (spectra + 8), LANES), jnp.float32),
            pltpu.VMEM((PART * width, 2 * C), jnp.bfloat16),
            pltpu.VMEM((CHUNK * PART, width), jnp.float32),
            pltpu.VMEM((steps, C // PAIR, GROUP, width), jnp.bfloat16),
            pltpu.SemaphoreType.DMA((groups,)),
            pltpu.SemaphoreType.DMA,
            pltpu.SemaphoreType.DMA((2, groups)),
            pltpu.SemaphoreType.DMA((2, groups)),
            pltpu.SemaphoreType.DMA((steps, devices)),
            pltpu.SemaphoreType.DMA((steps, devices)),
            pltpu.SemaphoreType.DMA((steps,)),
            pltpu.SemaphoreType.DMA((PEERS, steps)),
        ],
        compiler_params=pltpu.CompilerParams(
            collective_id=0, has_side_effects=True, vmem_limit_bytes=60 * 1024 * 1024
        ),
    )(voltages, jnp.asarray(dft_table()), delays, fringe, fringe_rate, filter_taps)


def gram_kernel(scale, late_count, spectra_ref, *refs):
    stn_count, tm_count, steps, pairs, size, width = spectra_ref.shape
    if late_count:
        real_ref, imag_ref, filled = refs[late_count + 2 :]
        stn, tm = lax.axis_index("stn"), lax.axis_index("tm")
        filled[...] = spectra_ref[...]
        for k in range(late_count):
            filled[jnp.bitwise_xor(stn, stn_count // 2), jnp.bitwise_xor(tm, k)] = refs[k][...]
    else:
        real_ref, imag_ref = refs
        filled = spectra_ref
    whole = stn_count * steps * PART
    lane = lax.broadcasted_iota(jnp.int32, (whole, width), 1)
    last = (((1,), (1,)), ((), ()))
    for channel in range(pairs * PAIR):
        place = channel % PAIR * PART
        pieces, turned_pieces = [], []
        for source in range(tm_count):
            piece = filled[:, source, :, channel // PAIR].astype(jnp.float32)[:, :, place : place + PART]
            piece = piece.reshape(whole, width)
            turned = pltpu.roll(piece, width // 2, 1)
            pieces.append(piece.astype(jnp.bfloat16))
            turned_pieces.append(jnp.where(lane < width // 2, turned, -turned).astype(jnp.bfloat16))
        rows = jnp.concatenate(pieces, axis=1)
        swapped = jnp.concatenate(turned_pieces, axis=1)
        real_ref[channel] = lax.dot_general(rows, rows, last, preferred_element_type=jnp.float32) * scale
        imag_ref[channel] = lax.dot_general(swapped, rows, last, preferred_element_type=jnp.float32) * scale


def grams(received, scale, first, count, late=(), begun=()):
    stn_count, tm_count, steps, pairs, size, width = received.shape
    whole = stn_count * steps * PART
    channels = pairs * PAIR
    step = PAIR
    base = first // step
    block = (stn_count, tm_count, steps, 1, size, width)
    result = jax.ShapeDtypeStruct((channels, whole, whole), jnp.float32)
    inner = tm_count * width
    return pl.pallas_call(
        functools.partial(gram_kernel, scale, len(late)),
        grid=(count // step,),
        in_specs=[pl.BlockSpec(block, lambda c: (0, 0, 0, base + c, 0, 0))]
        + [pl.BlockSpec((steps, 1, size, width), lambda c: (0, c, 0, 0))] * len(late)
        + [pl.BlockSpec(memory_space=pl.ANY)] * len(begun),
        out_specs=[pl.BlockSpec((step, whole, whole), lambda c: (base + c, 0, 0))] * 2,
        out_shape=[result, result],
        scratch_shapes=[pltpu.VMEM(block, received.dtype)] if late else [],
        input_output_aliases={1 + len(late) + i: i for i in range(len(begun))},
        compiler_params=pltpu.CompilerParams(vmem_limit_bytes=60 * 1024 * 1024),
        cost_estimate=pl.CostEstimate(
            flops=4 * count * whole * whole * inner,
            bytes_accessed=count * whole * (8 * whole + 2 * inner),
            transcendentals=0,
        ),
    )(received, *late, *begun)


def local(stn_count, tm_count, voltages, delays, fringe, fringe_rate, filter_taps):
    spectra = voltages.shape[2] // C
    devices = stn_count * tm_count
    received, *tails = spread_spectra(voltages, delays, fringe, fringe_rate, filter_taps, stn_count, tm_count)
    late = [
        lax.ppermute(tail, ("stn", "tm"), [(i, i ^ (devices // 2 + k)) for i in range(devices)])
        for k, tail in enumerate(tails)
    ]
    scale = 1.0 / (spectra * tm_count)
    channels, later = received.shape[3] * PAIR, tails[0].shape[1] * PAIR
    begun = grams(received, scale, 0, channels - later)
    real, imag = grams(received, scale, channels - later, later, late, begun)
    return (real, imag)


def solution(mesh):
    return jax.shard_map(
        functools.partial(local, mesh.shape["stn"], mesh.shape["tm"]),
        mesh=mesh,
        in_specs=(P(None, "stn", "tm"), P("stn"), P("stn"), P("stn"), P()),
        out_specs=(P(("stn", "tm"), None, None), P(("stn", "tm"), None, None)),
        check_vma=False,
    )
```

```python
import functools
import math

import jax
import jax.numpy as jnp
import numpy as np
from jax import lax
from jax.experimental import pallas as pl
from jax.experimental.pallas import tpu as pltpu
from jax.sharding import PartitionSpec as P

C = 1024
P_SIZE = 16
Q = 4096
DMAX = 2048

TWO_PI = 2.0 * math.pi
LANES = 128
GROUP = 16
PART = 8
PAIR = GROUP // PART
CHUNK = 256
STEP = 16
PEERS = 4
TAIL = 4
EARLY = DMAX // C
LATE = P_SIZE - 1
WIDE = P_SIZE + EARLY
MESH = pl.DeviceIdType.MESH


def dft_table():
    column = np.arange(C, dtype=np.int64)
    angles = (column[:, None] * column[None, :] % C).astype(np.float32) * np.float32(TWO_PI / C)
    both = np.concatenate([np.cos(angles), np.sin(angles)], axis=1)
    return both.astype(jnp.bfloat16)


def roll_left(tiles, amount):
    count = len(tiles)
    lane = lax.broadcasted_iota(jnp.int32, tiles[0].shape, 1)
    within = jnp.bitwise_and(amount, LANES - 1)
    source = jnp.bitwise_and(lane + within, LANES - 1)
    turned = [jnp.take_along_axis(tile, source, axis=1) for tile in tiles]
    line = [jnp.where(lane < LANES - within, turned[i], turned[(i + 1) % count]) for i in range(count)]
    step = 1
    while step < count:
        chosen = jnp.bitwise_and(amount, step * LANES) != 0
        line = [jnp.where(chosen, line[(i + step) % count], line[i]) for i in range(count)]
        step *= 2
    return line


def by_station(ref, first, index, shape):
    value = jnp.zeros(shape, jnp.int32)
    for i in range(PART):
        value = jnp.where(index == i, ref[first + i], value)
    return value


def spread_kernel(
    stn_count, tm_count, volt, table_ref, delay_ref, fringe_ref, rate_ref, taps_ref, recv, *rest
):
    tails = rest[:PEERS]
    (
        x, table, taps, lag, turn, mixed, rows, flat, send,
        load_sem, table_sem, early_sems, late_sems, send_sems, recv_sems, own_sems, tail_sems,
    ) = rest[PEERS:]
    stn, tm = lax.axis_index("stn"), lax.axis_index("tm")
    me = stn * tm_count + tm
    devices = stn_count * tm_count
    groups, steps = x.shape[0], send.shape[0]
    samples = volt.shape[2]
    spectra = samples // C
    each = C // devices
    per_chunk = CHUNK // each
    packed = each // PAIR
    chunks = C // CHUNK
    tiles = C // LANES
    apart = mixed.shape[0] // PART
    later = tails[0].shape[1]
    opposite = devices // 2

    def load(g):
        return pltpu.make_async_copy(
            volt.at[:, pl.ds(g * GROUP, GROUP), :],
            x.at[g, :, :, pl.ds(EARLY * C, samples)],
            load_sem.at[g],
        )

    def early(g):
        return pltpu.make_async_remote_copy(
            volt.at[:, pl.ds(g * GROUP, GROUP), pl.ds(samples - EARLY * C, EARLY * C)],
            x.at[g, :, :, pl.ds(0, EARLY * C)],
            early_sems.at[0, g], early_sems.at[1, g],
            device_id=(stn, lax.rem(tm + 1, tm_count)), device_id_type=MESH,
        )

    def late(g):
        return pltpu.make_async_remote_copy(
            volt.at[:, pl.ds(g * GROUP, GROUP), pl.ds(0, LATE * C)],
            x.at[g, :, :, pl.ds(EARLY * C + samples, LATE * C)],
            late_sems.at[0, g], late_sems.at[1, g],
            device_id=(stn, lax.rem(tm + tm_count - 1, tm_count)), device_id_type=MESH,
        )

    def spread(g, mask):
        other = jnp.bitwise_xor(me, mask)
        return pltpu.make_async_remote_copy(
            send.at[g, pl.ds(other * packed, packed)],
            recv.at[stn, tm, g],
            send_sems.at[g, mask], recv_sems.at[g, mask],
            device_id=(other // tm_count, lax.rem(other, tm_count)), device_id_type=MESH,
        )

    def spread_part(g, mask):
        other = jnp.bitwise_xor(me, mask)
        return pltpu.make_async_remote_copy(
            send.at[g, pl.ds(other * packed, packed - later)],
            recv.at[stn, tm, g, pl.ds(0, packed - later)],
            send_sems.at[g, mask], recv_sems.at[g, mask],
            device_id=(other // tm_count, lax.rem(other, tm_count)), device_id_type=MESH,
        )

    def both(mask, act, g):
        partly = jnp.logical_and(mask >= opposite, mask < opposite + PEERS)

        @pl.when(partly)
        def _():
            act(spread_part(g, mask))

        @pl.when(jnp.logical_not(partly))
        def _():
            act(spread(g, mask))

    def tail(g, k):
        other = jnp.bitwise_xor(me, opposite + k)
        return pltpu.make_async_copy(
            send.at[g, pl.ds(other * packed + packed - later, later)], tails[k].at[g], tail_sems.at[k, g]
        )

    def keep(g):
        return pltpu.make_async_copy(send.at[g, pl.ds(me * packed, packed)], recv.at[stn, tm, g], own_sems.at[g])

    whole_table = pltpu.make_async_copy(table_ref, table, table_sem)
    load(0).start()

    barrier = pltpu.get_barrier_semaphore()

    def greet(mask, carry):
        other = jnp.bitwise_xor(me, mask)
        pl.semaphore_signal(
            barrier, inc=1, device_id=(other // tm_count, lax.rem(other, tm_count)), device_id_type=MESH
        )
        return carry

    lax.fori_loop(1, devices, greet, 0)

    def reach(g):
        @pl.when(tm < tm_count - 1)
        def _():
            early(g).start()

        @pl.when(tm > 0)
        def _():
            late(g).start()

    def prepare(step):
        first_station = step * PART
        sub = lax.broadcasted_iota(jnp.int32, (8, LANES), 0)
        delay = by_station(delay_ref, first_station, sub, (8, LANES))
        lag[...] = delay
        for tap in range(P_SIZE):
            line = [
                jnp.broadcast_to(taps_ref[tap : tap + 1, i * LANES : (i + 1) * LANES], (8, LANES))
                for i in range(tiles)
            ]
            line = roll_left(line, jnp.bitwise_and(delay, C - 1))
            for i in range(tiles):
                taps[EARLY + tap, :, i * LANES : (i + 1) * LANES] = line[i]
        lane = lax.broadcasted_iota(jnp.int32, (8, LANES), 1)
        which = jnp.bitwise_and(lane, PART - 1)
        start = by_station(fringe_ref, first_station, which, (8, LANES)) - jnp.where(lane < PART, 0, Q // 4)
        rate = by_station(rate_ref, first_station, which, (8, LANES)) - (Q // C) * by_station(
            delay_ref, first_station, which, (8, LANES)
        )

        def angle(block, carry):
            first = pl.multiple_of(block * 32, 32)
            for more in range(0, 32, 8):
                phase_index = jnp.bitwise_and(start + rate * (sub + first + more), Q - 1)
                turn[pl.ds(first + more, 8), :] = jnp.cos(phase_index.astype(jnp.float32) * (TWO_PI / Q)) * (
                    1.0 / math.sqrt(C)
                )
            return carry

        lax.fori_loop(0, C // 32, angle, 0)

    for edge in list(range(EARLY)) + list(range(EARLY + P_SIZE, 2 * EARLY + P_SIZE)):
        taps[edge] = jnp.zeros((PART, C), jnp.float32)

    @pl.when(tm == 0)
    def _():
        x[:, :, :, 0 : EARLY * C] = jnp.zeros((groups, 2, GROUP, EARLY * C), x.dtype)

    @pl.when(tm == tm_count - 1)
    def _():
        for g in range(groups):
            x[g, :, :, EARLY * C + samples :] = jnp.zeros((2, GROUP, LATE * C), x.dtype)

    prepare(0)
    pl.semaphore_wait(barrier, devices - 1)
    reach(0)

    def one_step(step, carry):
        g, second = step // PAIR, lax.rem(step, PAIR)

        @pl.when(second == 0)
        def _():
            load(g).wait()

            @pl.when(g + 1 < groups)
            def _():
                load(g + 1).start()

        @pl.when(step == 0)
        def _():
            whole_table.start()

        def weigh(ranges, index, carry):
            part = index // tiles
            offset = pl.multiple_of(lax.rem(index, tiles) * LANES, LANES)
            lane = offset + lax.broadcasted_iota(jnp.int32, (8, LANES), 1)
            delay = lag[...]
            behind = lax.shift_right_logical(delay, C.bit_length() - 1) + jnp.where(
                lane >= C - jnp.bitwise_and(delay, C - 1), 1, 0
            )
            rolled = [taps[q, :, pl.ds(offset, LANES)] for q in range(WIDE + EARLY)]
            factor = []
            for q in range(WIDE):
                value = rolled[q]
                for back in range(1, EARLY + 1):
                    value = jnp.where(behind == back, rolled[q + back], value)
                factor.append(value)
            for base in [base for low, high in ranges for base in range(low, high, STEP)]:
                frames = []
                for j in range(STEP + WIDE - 1):
                    value = x[
                        g, part, :, pl.ds(pl.multiple_of((base + j) * C + offset, LANES), LANES)
                    ].astype(jnp.float32)
                    frames.append(jnp.where(second == 0, value[:PART], value[PART:]))
                for m in range(STEP):
                    total = factor[0] * frames[m]
                    for q in range(1, WIDE):
                        total = total + factor[q] * frames[m + q]
                    mixed[pl.ds(base + m, 8, stride=apart), :] = total
            sign = jnp.where(part == 0, -1.0, 1.0)
            same = pl.multiple_of(part * C + offset, LANES)
            cross = pl.multiple_of((1 - part) * C + offset, LANES)
            for s in range(PART):
                first = s * 2 * spectra
                for low, high in ranges:
                    value = mixed[s * apart + low : s * apart + high, :]
                    rows[first + low : first + high, pl.ds(same, LANES)] = value.astype(jnp.bfloat16)
                    rows[first + spectra + low : first + spectra + high, pl.ds(cross, LANES)] = (
                        value * sign
                    ).astype(jnp.bfloat16)
            return carry

        inner = (spectra - LATE) // STEP * STEP
        if inner > STEP:
            middle, ends = [(STEP, inner)], [(0, STEP), (inner, spectra)]
            lax.fori_loop(0, 2 * tiles, functools.partial(weigh, middle), 0)
        else:
            ends = [(0, spectra)]

        @pl.when(jnp.logical_and(second == 0, tm > 0))
        def _():
            early(g).wait_recv()

        @pl.when(jnp.logical_and(second == 0, tm < tm_count - 1))
        def _():
            late(g).wait_recv()

        lax.fori_loop(0, 2 * tiles, functools.partial(weigh, ends), 0)

        @pl.when(step == 0)
        def _():
            whole_table.wait()

        @pl.when(jnp.logical_and(second == PAIR - 1, g + 1 < groups))
        def _():
            reach(g + 1)

        def one_chunk(index, carry):
            near = lax.rem(index, 2)
            away = (1 - near) * (chunks // 2) + index // 2
            chunk = jnp.bitwise_xor(me // per_chunk, away)
            first = pl.multiple_of(chunk * CHUNK, CHUNK)
            left = table[pl.ds(first, CHUNK), :]
            width = 2 * spectra
            side = jnp.where(lax.broadcasted_iota(jnp.int32, (CHUNK, width), 1) < spectra, -1.0, 1.0)
            for s in range(0, PART, 2):
                product = lax.dot_general(
                    left, rows[s * width : (s + 2) * width, :], (((1,), (1,)), ((), ())),
                    preferred_element_type=jnp.float32,
                )
                for station in (s, s + 1):
                    value = product[:, (station - s) * width : (station - s + 1) * width]
                    cosine = turn[pl.ds(first, CHUNK), station : station + 1]
                    sine = turn[pl.ds(first, CHUNK), PART + station : PART + station + 1]
                    turned = value * cosine + pltpu.roll(value, spectra, 1) * (side * sine)
                    for c in range(0, CHUNK, 8):
                        flat[pl.ds(c * PART + station, 8, stride=PART), :] = turned[c : c + 8]

            def pack(block, carry):
                value = flat[pl.ds(pl.multiple_of(block * 128, 128), 128), :].astype(jnp.bfloat16)
                send[step, pl.ds(first // PAIR + block * (128 // GROUP), 128 // GROUP)] = value.reshape(
                    128 // GROUP, GROUP, width
                )
                return carry

            lax.fori_loop(0, CHUNK * PART // 128, pack, 0)

            @pl.when(index == 0)
            def _():
                for k in range(PEERS):
                    tail(step, k).start()

            def go(i, carry):
                mask = away * per_chunk + i

                @pl.when(jnp.logical_and(near == 1, step > 0))
                def _():
                    both((away + chunks // 2) * per_chunk + i, lambda copy: copy.start(), step)

                @pl.when(jnp.logical_and(mask > 0, jnp.logical_or(near == 1, step == 0)))
                def _():
                    both(mask, lambda copy: copy.start(), step)

                @pl.when(mask == 0)
                def _():
                    keep(step).start()

                return carry

            lax.fori_loop(0, per_chunk, go, 0)
            return carry

        lax.fori_loop(0, chunks, one_chunk, 0)

        @pl.when(step + 1 < steps)
        def _():
            prepare(step + 1)

        return carry

    lax.fori_loop(0, steps, one_step, 0)

    for g in range(steps):
        keep(g).wait()
        for k in range(PEERS):
            tail(g, k).wait()

        def come(mask, carry):
            both(mask, lambda copy: copy.wait(), g)
            return carry

        lax.fori_loop(1, devices, come, 0)

    @pl.when(tm > 0)
    def _():
        for g in range(groups):
            late(g).wait_send()

    @pl.when(tm < tm_count - 1)
    def _():
        for g in range(groups):
            early(g).wait_send()


def spread_spectra(voltages, delays, fringe, fringe_rate, filter_taps, stn_count, tm_count):
    stations, samples = voltages.shape[1:]
    spectra = samples // C
    groups = stations // GROUP
    devices = stn_count * tm_count
    each = C // devices
    width = 2 * spectra
    steps = groups * PAIR
    packed = each // PAIR
    later = packed // TAIL
    vmem = pl.BlockSpec(memory_space=pltpu.VMEM)
    smem = pl.BlockSpec(memory_space=pltpu.SMEM)
    hbm = pl.BlockSpec(memory_space=pl.ANY)
    return pl.pallas_call(
        functools.partial(spread_kernel, stn_count, tm_count),
        in_specs=[hbm, hbm, smem, smem, smem, vmem],
        out_specs=[hbm] * (1 + PEERS),
        out_shape=[jax.ShapeDtypeStruct((stn_count, tm_count, steps, packed, GROUP, width), jnp.bfloat16)]
        + [jax.ShapeDtypeStruct((steps, later, GROUP, width), jnp.bfloat16)] * PEERS,
        scratch_shapes=[
            pltpu.VMEM((groups, 2, GROUP, (EARLY + LATE) * C + samples), jnp.bfloat16),
            pltpu.VMEM((C, 2 * C), jnp.bfloat16),
            pltpu.VMEM((P_SIZE + 2 * EARLY, PART, C), jnp.float32),
            pltpu.VMEM((PART, LANES), jnp.int32),
            pltpu.VMEM((C, LANES), jnp.float32),
            pltpu.VMEM((PART * (spectra + 8), LANES), jnp.float32),
            pltpu.VMEM((PART * width, 2 * C), jnp.bfloat16),
            pltpu.VMEM((CHUNK * PART, width), jnp.float32),
            pltpu.VMEM((steps, C // PAIR, GROUP, width), jnp.bfloat16),
            pltpu.SemaphoreType.DMA((groups,)),
            pltpu.SemaphoreType.DMA,
            pltpu.SemaphoreType.DMA((2, groups)),
            pltpu.SemaphoreType.DMA((2, groups)),
            pltpu.SemaphoreType.DMA((steps, devices)),
            pltpu.SemaphoreType.DMA((steps, devices)),
            pltpu.SemaphoreType.DMA((steps,)),
            pltpu.SemaphoreType.DMA((PEERS, steps)),
        ],
        compiler_params=pltpu.CompilerParams(
            collective_id=0, has_side_effects=True, vmem_limit_bytes=60 * 1024 * 1024
        ),
    )(voltages, jnp.asarray(dft_table()), delays, fringe, fringe_rate, filter_taps)


def gram_kernel(scale, late_count, spectra_ref, *refs):
    stn_count, tm_count, steps, pairs, size, width = spectra_ref.shape
    if late_count:
        real_ref, imag_ref, filled = refs[late_count + 2 :]
        stn, tm = lax.axis_index("stn"), lax.axis_index("tm")
        filled[...] = spectra_ref[...]
        for k in range(late_count):
            filled[jnp.bitwise_xor(stn, stn_count // 2), jnp.bitwise_xor(tm, k)] = refs[k][...]
    else:
        real_ref, imag_ref = refs
        filled = spectra_ref
    whole = stn_count * steps * PART
    lane = lax.broadcasted_iota(jnp.int32, (whole, width), 1)
    last = (((1,), (1,)), ((), ()))
    for channel in range(pairs * PAIR):
        place = channel % PAIR * PART
        pieces, turned_pieces = [], []
        for source in range(tm_count):
            piece = filled[:, source, :, channel // PAIR].astype(jnp.float32)[:, :, place : place + PART]
            piece = piece.reshape(whole, width)
            turned = pltpu.roll(piece, width // 2, 1)
            pieces.append(piece.astype(jnp.bfloat16))
            turned_pieces.append(jnp.where(lane < width // 2, turned, -turned).astype(jnp.bfloat16))
        rows = jnp.concatenate(pieces, axis=1)
        swapped = jnp.concatenate(turned_pieces, axis=1)
        real_ref[channel] = lax.dot_general(rows, rows, last, preferred_element_type=jnp.float32) * scale
        imag_ref[channel] = lax.dot_general(swapped, rows, last, preferred_element_type=jnp.float32) * scale


def grams(received, scale, first, count, late=(), begun=()):
    stn_count, tm_count, steps, pairs, size, width = received.shape
    whole = stn_count * steps * PART
    channels = pairs * PAIR
    step = PAIR
    base = first // step
    block = (stn_count, tm_count, steps, 1, size, width)
    result = jax.ShapeDtypeStruct((channels, whole, whole), jnp.float32)
    inner = tm_count * width
    return pl.pallas_call(
        functools.partial(gram_kernel, scale, len(late)),
        grid=(count // step,),
        in_specs=[pl.BlockSpec(block, lambda c: (0, 0, 0, base + c, 0, 0))]
        + [pl.BlockSpec((steps, 1, size, width), lambda c: (0, c, 0, 0))] * len(late)
        + [pl.BlockSpec(memory_space=pl.ANY)] * len(begun),
        out_specs=[pl.BlockSpec((step, whole, whole), lambda c: (base + c, 0, 0))] * 2,
        out_shape=[result, result],
        scratch_shapes=[pltpu.VMEM(block, received.dtype)] if late else [],
        input_output_aliases={1 + len(late) + i: i for i in range(len(begun))},
        compiler_params=pltpu.CompilerParams(vmem_limit_bytes=60 * 1024 * 1024),
        cost_estimate=pl.CostEstimate(
            flops=4 * count * whole * whole * inner,
            bytes_accessed=count * whole * (8 * whole + 2 * inner),
            transcendentals=0,
        ),
    )(received, *late, *begun)


def local(stn_count, tm_count, voltages, delays, fringe, fringe_rate, filter_taps):
    spectra = voltages.shape[2] // C
    devices = stn_count * tm_count
    received, *tails = spread_spectra(voltages, delays, fringe, fringe_rate, filter_taps, stn_count, tm_count)
    late = [
        lax.ppermute(tail, ("stn", "tm"), [(i, i ^ (devices // 2 + k)) for i in range(devices)])
        for k, tail in enumerate(tails)
    ]
    scale = 1.0 / (spectra * tm_count)
    channels, later = received.shape[3] * PAIR, tails[0].shape[1] * PAIR
    begun = grams(received, scale, 0, channels - later)
    real, imag = grams(received, scale, channels - later, later, late, begun)
    return (real, imag)


def solution(mesh):
    return jax.shard_map(
        functools.partial(local, mesh.shape["stn"], mesh.shape["tm"]),
        mesh=mesh,
        in_specs=(P(None, "stn", "tm"), P("stn"), P("stn"), P("stn"), P()),
        out_specs=(P(("stn", "tm"), None, None), P(("stn", "tm"), None, None)),
        check_vma=False,
    )
```

```python
import functools
import math

import jax
import jax.numpy as jnp
import numpy as np
from jax import lax
from jax.experimental import pallas as pl
from jax.experimental.pallas import tpu as pltpu
from jax.sharding import PartitionSpec as P

C = 1024
P_SIZE = 16
Q = 4096
DMAX = 2048

TWO_PI = 2.0 * math.pi
LANES = 128
GROUP = 16
PART = 8
PAIR = GROUP // PART
CHUNK = 256
STEP = 16
PEERS = 4
TAIL = 4
EARLY = DMAX // C
LATE = P_SIZE - 1
WIDE = P_SIZE + EARLY
MESH = pl.DeviceIdType.MESH


def dft_table():
    column = np.arange(C, dtype=np.int64)
    angles = (column[:, None] * column[None, :] % C).astype(np.float32) * np.float32(TWO_PI / C)
    both = np.concatenate([np.cos(angles), np.sin(angles)], axis=1)
    return both.astype(jnp.bfloat16)


def roll_left(tiles, amount):
    count = len(tiles)
    lane = lax.broadcasted_iota(jnp.int32, tiles[0].shape, 1)
    within = jnp.bitwise_and(amount, LANES - 1)
    source = jnp.bitwise_and(lane + within, LANES - 1)
    turned = [jnp.take_along_axis(tile, source, axis=1) for tile in tiles]
    line = [jnp.where(lane < LANES - within, turned[i], turned[(i + 1) % count]) for i in range(count)]
    step = 1
    while step < count:
        chosen = jnp.bitwise_and(amount, step * LANES) != 0
        line = [jnp.where(chosen, line[(i + step) % count], line[i]) for i in range(count)]
        step *= 2
    return line


def by_station(ref, first, index, shape):
    value = jnp.zeros(shape, jnp.int32)
    for i in range(PART):
        value = jnp.where(index == i, ref[first + i], value)
    return value


def spread_kernel(
    stn_count, tm_count, volt, table_ref, delay_ref, fringe_ref, rate_ref, taps_ref, recv, *rest
):
    tails = rest[:PEERS]
    (
        x, table, taps, lag, turn, mixed, rows, flat, send,
        load_sem, table_sem, early_sems, late_sems, send_sems, recv_sems, own_sems, tail_sems,
    ) = rest[PEERS:]
    stn, tm = lax.axis_index("stn"), lax.axis_index("tm")
    me = stn * tm_count + tm
    devices = stn_count * tm_count
    groups, steps = x.shape[0], send.shape[0]
    samples = volt.shape[2]
    spectra = samples // C
    each = C // devices
    per_chunk = CHUNK // each
    packed = each // PAIR
    chunks = C // CHUNK
    tiles = C // LANES
    apart = mixed.shape[0] // PART
    later = tails[0].shape[1]
    opposite = devices // 2

    def load(g):
        return pltpu.make_async_copy(
            volt.at[:, pl.ds(g * GROUP, GROUP), :],
            x.at[g, :, :, pl.ds(EARLY * C, samples)],
            load_sem.at[g],
        )

    def early(g):
        return pltpu.make_async_remote_copy(
            volt.at[:, pl.ds(g * GROUP, GROUP), pl.ds(samples - EARLY * C, EARLY * C)],
            x.at[g, :, :, pl.ds(0, EARLY * C)],
            early_sems.at[0, g], early_sems.at[1, g],
            device_id=(stn, lax.rem(tm + 1, tm_count)), device_id_type=MESH,
        )

    def late(g):
        return pltpu.make_async_remote_copy(
            volt.at[:, pl.ds(g * GROUP, GROUP), pl.ds(0, LATE * C)],
            x.at[g, :, :, pl.ds(EARLY * C + samples, LATE * C)],
            late_sems.at[0, g], late_sems.at[1, g],
            device_id=(stn, lax.rem(tm + tm_count - 1, tm_count)), device_id_type=MESH,
        )

    def spread(g, mask):
        other = jnp.bitwise_xor(me, mask)
        return pltpu.make_async_remote_copy(
            send.at[g, pl.ds(other * packed, packed)],
            recv.at[stn, tm, g],
            send_sems.at[g, mask], recv_sems.at[g, mask],
            device_id=(other // tm_count, lax.rem(other, tm_count)), device_id_type=MESH,
        )

    def spread_part(g, mask):
        other = jnp.bitwise_xor(me, mask)
        return pltpu.make_async_remote_copy(
            send.at[g, pl.ds(other * packed, packed - later)],
            recv.at[stn, tm, g, pl.ds(0, packed - later)],
            send_sems.at[g, mask], recv_sems.at[g, mask],
            device_id=(other // tm_count, lax.rem(other, tm_count)), device_id_type=MESH,
        )

    def both(mask, act, g):
        partly = jnp.logical_and(mask >= opposite, mask < opposite + PEERS)

        @pl.when(partly)
        def _():
            act(spread_part(g, mask))

        @pl.when(jnp.logical_not(partly))
        def _():
            act(spread(g, mask))

    def tail(g, k):
        other = jnp.bitwise_xor(me, opposite + k)
        return pltpu.make_async_copy(
            send.at[g, pl.ds(other * packed + packed - later, later)], tails[k].at[g], tail_sems.at[k, g]
        )

    def keep(g):
        return pltpu.make_async_copy(send.at[g, pl.ds(me * packed, packed)], recv.at[stn, tm, g], own_sems.at[g])

    whole_table = pltpu.make_async_copy(table_ref, table, table_sem)
    load(0).start()

    barrier = pltpu.get_barrier_semaphore()

    def greet(mask, carry):
        other = jnp.bitwise_xor(me, mask)
        pl.semaphore_signal(
            barrier, inc=1, device_id=(other // tm_count, lax.rem(other, tm_count)), device_id_type=MESH
        )
        return carry

    lax.fori_loop(1, devices, greet, 0)

    def reach(g):
        @pl.when(tm < tm_count - 1)
        def _():
            early(g).start()

        @pl.when(tm > 0)
        def _():
            late(g).start()

    def prepare(step):
        first_station = step * PART
        sub = lax.broadcasted_iota(jnp.int32, (8, LANES), 0)
        delay = by_station(delay_ref, first_station, sub, (8, LANES))
        lag[...] = delay
        for tap in range(P_SIZE):
            line = [
                jnp.broadcast_to(taps_ref[tap : tap + 1, i * LANES : (i + 1) * LANES], (8, LANES))
                for i in range(tiles)
            ]
            line = roll_left(line, jnp.bitwise_and(delay, C - 1))
            for i in range(tiles):
                taps[EARLY + tap, :, i * LANES : (i + 1) * LANES] = line[i]
        lane = lax.broadcasted_iota(jnp.int32, (8, LANES), 1)
        which = jnp.bitwise_and(lane, PART - 1)
        start = by_station(fringe_ref, first_station, which, (8, LANES)) - jnp.where(lane < PART, 0, Q // 4)
        rate = by_station(rate_ref, first_station, which, (8, LANES)) - (Q // C) * by_station(
            delay_ref, first_station, which, (8, LANES)
        )

        def angle(block, carry):
            first = pl.multiple_of(block * 32, 32)
            for more in range(0, 32, 8):
                phase_index = jnp.bitwise_and(start + rate * (sub + first + more), Q - 1)
                turn[pl.ds(first + more, 8), :] = jnp.cos(phase_index.astype(jnp.float32) * (TWO_PI / Q)) * (
                    1.0 / math.sqrt(C)
                )
            return carry

        lax.fori_loop(0, C // 32, angle, 0)

    for edge in list(range(EARLY)) + list(range(EARLY + P_SIZE, 2 * EARLY + P_SIZE)):
        taps[edge] = jnp.zeros((PART, C), jnp.float32)

    @pl.when(tm == 0)
    def _():
        x[:, :, :, 0 : EARLY * C] = jnp.zeros((groups, 2, GROUP, EARLY * C), x.dtype)

    @pl.when(tm == tm_count - 1)
    def _():
        for g in range(groups):
            x[g, :, :, EARLY * C + samples :] = jnp.zeros((2, GROUP, LATE * C), x.dtype)

    prepare(0)
    pl.semaphore_wait(barrier, devices - 1)
    reach(0)

    def one_step(step, carry):
        g, second = step // PAIR, lax.rem(step, PAIR)

        @pl.when(second == 0)
        def _():
            load(g).wait()

            @pl.when(g + 1 < groups)
            def _():
                load(g + 1).start()

        @pl.when(step == 0)
        def _():
            whole_table.start()

        def weigh(ranges, index, carry):
            part = index // tiles
            offset = pl.multiple_of(lax.rem(index, tiles) * LANES, LANES)
            lane = offset + lax.broadcasted_iota(jnp.int32, (8, LANES), 1)
            delay = lag[...]
            behind = lax.shift_right_logical(delay, C.bit_length() - 1) + jnp.where(
                lane >= C - jnp.bitwise_and(delay, C - 1), 1, 0
            )
            rolled = [taps[q, :, pl.ds(offset, LANES)] for q in range(WIDE + EARLY)]
            factor = []
            for q in range(WIDE):
                value = rolled[q]
                for back in range(1, EARLY + 1):
                    value = jnp.where(behind == back, rolled[q + back], value)
                factor.append(value)
            for base in [base for low, high in ranges for base in range(low, high, STEP)]:
                frames = []
                for j in range(STEP + WIDE - 1):
                    value = x[
                        g, part, :, pl.ds(pl.multiple_of((base + j) * C + offset, LANES), LANES)
                    ].astype(jnp.float32)
                    frames.append(jnp.where(second == 0, value[:PART], value[PART:]))
                for m in range(STEP):
                    total = factor[0] * frames[m]
                    for q in range(1, WIDE):
                        total = total + factor[q] * frames[m + q]
                    mixed[pl.ds(base + m, 8, stride=apart), :] = total
            sign = jnp.where(part == 0, -1.0, 1.0)
            same = pl.multiple_of(part * C + offset, LANES)
            cross = pl.multiple_of((1 - part) * C + offset, LANES)
            for s in range(PART):
                first = s * 2 * spectra
                for low, high in ranges:
                    value = mixed[s * apart + low : s * apart + high, :]
                    rows[first + low : first + high, pl.ds(same, LANES)] = value.astype(jnp.bfloat16)
                    rows[first + spectra + low : first + spectra + high, pl.ds(cross, LANES)] = (
                        value * sign
                    ).astype(jnp.bfloat16)
            return carry

        inner = (spectra - LATE) // STEP * STEP
        if inner > STEP:
            middle, ends = [(STEP, inner)], [(0, STEP), (inner, spectra)]
            lax.fori_loop(0, 2 * tiles, functools.partial(weigh, middle), 0)
        else:
            ends = [(0, spectra)]

        @pl.when(jnp.logical_and(second == 0, tm > 0))
        def _():
            early(g).wait_recv()

        @pl.when(jnp.logical_and(second == 0, tm < tm_count - 1))
        def _():
            late(g).wait_recv()

        lax.fori_loop(0, 2 * tiles, functools.partial(weigh, ends), 0)

        @pl.when(step == 0)
        def _():
            whole_table.wait()

        @pl.when(jnp.logical_and(second == PAIR - 1, g + 1 < groups))
        def _():
            reach(g + 1)

        def one_chunk(index, carry):
            near = lax.rem(index, 2)
            away = (1 - near) * (chunks // 2) + index // 2
            chunk = jnp.bitwise_xor(me // per_chunk, away)
            first = pl.multiple_of(chunk * CHUNK, CHUNK)
            left = table[pl.ds(first, CHUNK), :]
            width = 2 * spectra
            side = jnp.where(lax.broadcasted_iota(jnp.int32, (CHUNK, width), 1) < spectra, -1.0, 1.0)
            for s in range(0, PART, 2):
                product = lax.dot_general(
                    left, rows[s * width : (s + 2) * width, :], (((1,), (1,)), ((), ())),
                    preferred_element_type=jnp.float32,
                )
                for station in (s, s + 1):
                    value = product[:, (station - s) * width : (station - s + 1) * width]
                    cosine = turn[pl.ds(first, CHUNK), station : station + 1]
                    sine = turn[pl.ds(first, CHUNK), PART + station : PART + station + 1]
                    turned = value * cosine + pltpu.roll(value, spectra, 1) * (side * sine)
                    for c in range(0, CHUNK, 8):
                        flat[pl.ds(c * PART + station, 8, stride=PART), :] = turned[c : c + 8]

            def pack(block, carry):
                value = flat[pl.ds(pl.multiple_of(block * 128, 128), 128), :].astype(jnp.bfloat16)
                send[step, pl.ds(first // PAIR + block * (128 // GROUP), 128 // GROUP)] = value.reshape(
                    128 // GROUP, GROUP, width
                )
                return carry

            lax.fori_loop(0, CHUNK * PART // 128, pack, 0)

            @pl.when(index == 0)
            def _():
                for k in range(PEERS):
                    tail(step, k).start()

            def go(i, carry):
                mask = away * per_chunk + i

                @pl.when(jnp.logical_and(near == 1, step > 0))
                def _():
                    both((away + chunks // 2) * per_chunk + i, lambda copy: copy.start(), step)

                @pl.when(jnp.logical_and(mask > 0, jnp.logical_or(near == 1, step == 0)))
                def _():
                    both(mask, lambda copy: copy.start(), step)

                @pl.when(mask == 0)
                def _():
                    keep(step).start()

                return carry

            lax.fori_loop(0, per_chunk, go, 0)
            return carry

        lax.fori_loop(0, chunks, one_chunk, 0)

        @pl.when(step + 1 < steps)
        def _():
            prepare(step + 1)

        return carry

    lax.fori_loop(0, steps, one_step, 0)

    for g in range(steps):
        keep(g).wait()
        for k in range(PEERS):
            tail(g, k).wait()

        def come(mask, carry):
            both(mask, lambda copy: copy.wait(), g)
            return carry

        lax.fori_loop(1, devices, come, 0)

    @pl.when(tm > 0)
    def _():
        for g in range(groups):
            late(g).wait_send()

    @pl.when(tm < tm_count - 1)
    def _():
        for g in range(groups):
            early(g).wait_send()


def spread_spectra(voltages, delays, fringe, fringe_rate, filter_taps, stn_count, tm_count):
    stations, samples = voltages.shape[1:]
    spectra = samples // C
    groups = stations // GROUP
    devices = stn_count * tm_count
    each = C // devices
    width = 2 * spectra
    steps = groups * PAIR
    packed = each // PAIR
    later = packed // TAIL
    vmem = pl.BlockSpec(memory_space=pltpu.VMEM)
    smem = pl.BlockSpec(memory_space=pltpu.SMEM)
    hbm = pl.BlockSpec(memory_space=pl.ANY)
    return pl.pallas_call(
        functools.partial(spread_kernel, stn_count, tm_count),
        in_specs=[hbm, hbm, smem, smem, smem, vmem],
        out_specs=[hbm] * (1 + PEERS),
        out_shape=[jax.ShapeDtypeStruct((stn_count, tm_count, steps, packed, GROUP, width), jnp.bfloat16)]
        + [jax.ShapeDtypeStruct((steps, later, GROUP, width), jnp.bfloat16)] * PEERS,
        scratch_shapes=[
            pltpu.VMEM((groups, 2, GROUP, (EARLY + LATE) * C + samples), jnp.bfloat16),
            pltpu.VMEM((C, 2 * C), jnp.bfloat16),
            pltpu.VMEM((P_SIZE + 2 * EARLY, PART, C), jnp.float32),
            pltpu.VMEM((PART, LANES), jnp.int32),
            pltpu.VMEM((C, LANES), jnp.float32),
            pltpu.VMEM((PART * (spectra + 8), LANES), jnp.float32),
            pltpu.VMEM((PART * width, 2 * C), jnp.bfloat16),
            pltpu.VMEM((CHUNK * PART, width), jnp.float32),
            pltpu.VMEM((steps, C // PAIR, GROUP, width), jnp.bfloat16),
            pltpu.SemaphoreType.DMA((groups,)),
            pltpu.SemaphoreType.DMA,
            pltpu.SemaphoreType.DMA((2, groups)),
            pltpu.SemaphoreType.DMA((2, groups)),
            pltpu.SemaphoreType.DMA((steps, devices)),
            pltpu.SemaphoreType.DMA((steps, devices)),
            pltpu.SemaphoreType.DMA((steps,)),
            pltpu.SemaphoreType.DMA((PEERS, steps)),
        ],
        compiler_params=pltpu.CompilerParams(
            collective_id=0, has_side_effects=True, vmem_limit_bytes=60 * 1024 * 1024
        ),
    )(voltages, jnp.asarray(dft_table()), delays, fringe, fringe_rate, filter_taps)


def gram_kernel(scale, late_count, spectra_ref, *refs):
    stn_count, tm_count, steps, pairs, size, width = spectra_ref.shape
    if late_count:
        real_ref, imag_ref, filled = refs[late_count + 2 :]
        stn, tm = lax.axis_index("stn"), lax.axis_index("tm")
        filled[...] = spectra_ref[...]
        for k in range(late_count):
            filled[jnp.bitwise_xor(stn, stn_count // 2), jnp.bitwise_xor(tm, k)] = refs[k][...]
    else:
        real_ref, imag_ref = refs
        filled = spectra_ref
    whole = stn_count * steps * PART
    lane = lax.broadcasted_iota(jnp.int32, (whole, width), 1)
    last = (((1,), (1,)), ((), ()))
    for channel in range(pairs * PAIR):
        place = channel % PAIR * PART
        pieces, turned_pieces = [], []
        for source in range(tm_count):
            piece = filled[:, source, :, channel // PAIR].astype(jnp.float32)[:, :, place : place + PART]
            piece = piece.reshape(whole, width)
            turned = pltpu.roll(piece, width // 2, 1)
            pieces.append(piece.astype(jnp.bfloat16))
            turned_pieces.append(jnp.where(lane < width // 2, turned, -turned).astype(jnp.bfloat16))
        rows = jnp.concatenate(pieces, axis=1)
        swapped = jnp.concatenate(turned_pieces, axis=1)
        real_ref[channel] = lax.dot_general(rows, rows, last, preferred_element_type=jnp.float32) * scale
        imag_ref[channel] = lax.dot_general(swapped, rows, last, preferred_element_type=jnp.float32) * scale


def grams(received, scale, first, count, late=(), begun=()):
    stn_count, tm_count, steps, pairs, size, width = received.shape
    whole = stn_count * steps * PART
    channels = pairs * PAIR
    both = 1 if late or count % (2 * PAIR) else 2
    step = both * PAIR
    base = first // step
    block = (stn_count, tm_count, steps, both, size, width)
    result = jax.ShapeDtypeStruct((channels, whole, whole), jnp.float32)
    inner = tm_count * width
    return pl.pallas_call(
        functools.partial(gram_kernel, scale, len(late)),
        grid=(count // step,),
        in_specs=[pl.BlockSpec(block, lambda c: (0, 0, 0, base + c, 0, 0))]
        + [pl.BlockSpec((steps, 1, size, width), lambda c: (0, c, 0, 0))] * len(late)
        + [pl.BlockSpec(memory_space=pl.ANY)] * len(begun),
        out_specs=[pl.BlockSpec((step, whole, whole), lambda c: (base + c, 0, 0))] * 2,
        out_shape=[result, result],
        scratch_shapes=[pltpu.VMEM(block, received.dtype)] if late else [],
        input_output_aliases={1 + len(late) + i: i for i in range(len(begun))},
        compiler_params=pltpu.CompilerParams(vmem_limit_bytes=60 * 1024 * 1024),
        cost_estimate=pl.CostEstimate(
            flops=4 * count * whole * whole * inner,
            bytes_accessed=count * whole * (8 * whole + 2 * inner),
            transcendentals=0,
        ),
    )(received, *late, *begun)


def local(stn_count, tm_count, voltages, delays, fringe, fringe_rate, filter_taps):
    spectra = voltages.shape[2] // C
    devices = stn_count * tm_count
    received, *tails = spread_spectra(voltages, delays, fringe, fringe_rate, filter_taps, stn_count, tm_count)
    late = [
        lax.ppermute(tail, ("stn", "tm"), [(i, i ^ (devices // 2 + k)) for i in range(devices)])
        for k, tail in enumerate(tails)
    ]
    scale = 1.0 / (spectra * tm_count)
    channels, later = received.shape[3] * PAIR, tails[0].shape[1] * PAIR
    begun = grams(received, scale, 0, channels - later)
    real, imag = grams(received, scale, channels - later, later, late, begun)
    return (real, imag)


def solution(mesh):
    return jax.shard_map(
        functools.partial(local, mesh.shape["stn"], mesh.shape["tm"]),
        mesh=mesh,
        in_specs=(P(None, "stn", "tm"), P("stn"), P("stn"), P("stn"), P()),
        out_specs=(P(("stn", "tm"), None, None), P(("stn", "tm"), None, None)),
        check_vma=False,
    )
```
